256 devices in a mesh: mem: 4 (over y), col: 64 (over z, x, core).
Axes of the slice: x: 4, y: 4, z: 8, core: 2. Of those that a mesh axis runs over, the one named last changes fastest.
Arguments:
- increment: float32 [8, 1048576], P(None, 'col'), may hold values from -6 to 6
- ensemble: bfloat16 [64, 8, 1048576], P('mem', None, 'col'), may hold values from -15 to 15
- climate: float32 [8, 1048576], P(None, 'col'), may hold values from 0.5 to 2
- restrict_dest: int32 [16384, 1], replicated, may hold values from 0 to 63; in each aligned block of 256 rows (0 to 255, 256 to 511, ...) at most 8 rows name the same one
- restrict_local: int32 [16384], replicated, may hold values from 0 to 255
- restrict_weight: float32 [1048576], P('col'), may hold values from 0.05 to 0.2
- conv_blocks: bfloat16 [128, 4, 128, 128], P('col'), may hold values from -0.25 to 0.25
- neighbours: int32 [128, 4], P('col'), may hold values from 0 to 127, as said below
- interp_dest: int32 [16384, 2], replicated, may hold values from 0 to 63, all different within a row; in each aligned block of 256 rows (0 to 255, 256 to 511, ...) at most 16 rows name the same one
- interp_local: int32 [16384, 2], replicated, may hold values from 0 to 255
- interp_weight: float32 [2, 1048576], P(None, 'col'), may hold values from 0.2 to 1
Outputs:
- once_applied: float32 [8, 1048576], P(None, 'col')
- twice_applied: float32 [8, 1048576], P(None, 'col')
The draws below stay inside these ranges and needn't reach their ends.
Inputs may be any that keep to these rules, and one draw needn't show every extreme that they name: `restrict_dest`: in each aligned block of 256 rows (the tiles of one index of col) no device number appears in more than 8 rows. `interp_dest`: the two entries of a row differ. In each aligned block of 256 rows no device number appears in more than 16 rows. `neighbours`: the 4 entries of row b are distinct blocks among b - 2 to b + 2, taken modulo 128.
All inputs are finite; a program needn't handle non-finite values.
Results may differ from the reference program's by a relative error of at most 0.008.
Values may be sent and summed in bfloat16 or wider, within the bound.
A program may use at most 128 MiB of HBM per device.

```python
import math
import jax
import jax.numpy as jnp
import numpy as np
from jax import lax

LEVELS = 8
TILE = 64
BLK_DEV = 2
NEIGH = 4
COARSE_DEV = 256
CBLK = 128
CAP = 8
MEMBERS = 64
FINE = 1048576
COARSE = 16384
BLOCKS = 128
N_COL = 64


def draw_neighbours(key, part):
    choices_count = 2 * BLK_DEV + 1
    scores = jax.random.randint(key, (BLOCKS, choices_count), 0, 1 << 20) * choices_count + jnp.arange(choices_count, dtype=jnp.int32)[None, :]
    ordering = jnp.argsort(scores, axis=1, stable=True)[:, :NEIGH]
    offsets = ordering - BLK_DEV
    return ((jnp.arange(BLOCKS, dtype=jnp.int32)[:, None] + offsets) % BLOCKS).astype(jnp.int32)


def touch_ends(values, stream_key, low, top_value):
    spot = [jax.random.randint(jax.random.fold_in(stream_key, axis), (), 0, length) for axis, length in enumerate(values.shape)]
    main_axis = values.shape.index(max(values.shape))
    neighbour = spot[:main_axis] + [(spot[main_axis] + 1) % values.shape[main_axis]] + spot[main_axis + 1:]
    return values.at[tuple(spot)].set(low).at[tuple(neighbour)].set(top_value)


def shard_levels(key, extent, cuts, smallest, largest):
    def one(position, parts):
        steps = jax.random.uniform(jax.random.fold_in(jax.random.fold_in(key, 6), position), (parts,), jnp.float32, smallest / len(cuts), largest / len(cuts))
        return jnp.repeat(jnp.exp(steps), extent[position] // parts).reshape((-1,) + (1,) * (len(extent) - position - 1))

    level = one(*cuts[0])
    for cut in cuts[1:]:
        level = level * one(*cut)
    return level


def deal_out(own_key, own, number, rows, number_of, top, limit, skew):
    ranking = jax.random.permutation(own_key, number_of)
    crowded, ordinary = load_shares(number_of, rows * top, limit, skew, True), load_shares(number_of, rows * top, limit, skew, False)
    places = jnp.arange(number_of)

    def named(sizes, turn):
        used = int((sizes > 0).sum())
        fixed = max(1, used // 4)
        moved = fixed + (places - fixed + turn * (used - fixed)) % max(1, number_of - fixed)
        return jnp.zeros((number_of,), jnp.int32).at[ranking[jnp.where(places < fixed, places, moved)]].set(jnp.asarray(sizes, jnp.int32))

    sizes = jnp.where(number % 4 == 0, named(crowded, number // 4), named(ordinary, number - number // 4 - 1))
    mixed = jax.random.permutation(jax.random.fold_in(own, 3), number_of)
    giver, taker = mixed[0:number_of // 2 * 2:2], mixed[1:number_of // 2 * 2:2]
    room = jnp.minimum(sizes[giver] - 1, limit - sizes[taker]) // 2
    room = jnp.where((giver == ranking[0]) | (taker == ranking[0]) | (sizes[taker] == 0), 0, jnp.maximum(room, 0))
    moved = jax.random.randint(jax.random.fold_in(own, 4), (number_of // 2,), 0, 1 << 20) % (room + 1)
    sizes = sizes.at[giver].add(-moved).at[taker].add(moved)
    items = jnp.searchsorted(jnp.cumsum(sizes), jnp.arange(rows * top), side="right").astype(jnp.int32)
    listing = items.reshape(top, rows).T
    listing = listing[jax.random.permutation(jax.random.fold_in(own, 1), rows)]
    turn = jax.random.randint(jax.random.fold_in(own, 2), (rows, 1), 0, top)
    return jnp.take_along_axis(listing, (jnp.arange(top)[None, :] + turn) % top, axis=1)


def load_shares(count, total, most, skew, full):
    weights = [(1 << 20) // math.isqrt(rank ** skew) + 1 for rank in range(1, count + 1)]
    largest = most if full else min(most, max(-(-total // count), total * weights[0] // sum(weights)))
    least = 1 if total - largest >= count - 1 else 0
    given, rest = [largest] + [least] * (count - 1), total - largest - least * (count - 1)
    while rest > 0:
        candidates = [i for i in range(1, count) if given[i] < largest] or [i for i in range(1, count) if given[i] < most]
        mass, remaining = sum([weights[i] for i in candidates]), rest
        for i in candidates:
            extra = min(most - given[i], max(1, remaining * weights[i] // mass), rest)
            given[i] = given[i] + extra
            rest = rest - extra
    return np.array(given)


def scatter_about(own_key, shape, spread, limit, split=(), kind=jnp.bfloat16):
    gain = shard_levels(own_key, shape, split, -0.22, 0.18) if split else 1.0
    result = jax.random.normal(own_key, shape, jnp.float32) * spread * gain
    return jnp.minimum(jnp.maximum(result, -limit), limit).astype(kind)


def setup_inputs(seed: int = 0) -> dict:
    keys = jax.random.split(jax.random.key(seed), 12)
    increment = scatter_about(keys[0], (LEVELS, FINE), 1.0, 6.0, ((1, 64),), jnp.float32)
    ensemble = scatter_about(keys[1], (MEMBERS, LEVELS, FINE), 2.5, 15.0, ((0, 4), (2, 64)))
    climate = jnp.clip(jnp.exp(math.log(2.0) - 1.3862944 * jax.random.uniform(keys[2], (LEVELS, FINE), jnp.float32) ** shard_levels(keys[2], (LEVELS, FINE), ((1, 64),), -0.2, 0.2)), 0.5, 2.0)
    restrict_dest_keys = jax.random.split(jax.random.fold_in(keys[3], 1), COARSE // COARSE_DEV)
    restrict_dest_turns = jax.random.permutation(jax.random.fold_in(keys[3], 3), COARSE // COARSE_DEV)
    restrict_dest = jax.vmap(lambda own, number: deal_out(jax.random.fold_in(keys[3], 2), own, number, COARSE_DEV, N_COL, 1, CAP, 2))(restrict_dest_keys, restrict_dest_turns).reshape((COARSE, 1))
    restrict_local = touch_ends(jax.random.randint(keys[4], (COARSE,), 0, COARSE_DEV), jax.random.fold_in(keys[4], 1), 0, COARSE_DEV - 1).astype(jnp.int32)
    restrict_weight = jnp.clip(jnp.exp(math.log(0.2) - 1.3862944 * jax.random.uniform(keys[5], (FINE,), jnp.float32) ** shard_levels(keys[5], (FINE,), ((0, 64),), -0.2, 0.2)), 0.05, 0.2)
    conv_blocks = scatter_about(keys[6], (BLOCKS, NEIGH, CBLK, CBLK), (NEIGH * CBLK) ** -0.5, 0.25, ((0, 64),))
    neighbours = draw_neighbours(jax.random.fold_in(keys[11], 71), 0)
    interp_dest_keys = jax.random.split(jax.random.fold_in(keys[8], 1), COARSE // COARSE_DEV)
    interp_dest_turns = jax.random.permutation(jax.random.fold_in(keys[8], 3), COARSE // COARSE_DEV)
    interp_dest = jax.vmap(lambda own, number: deal_out(jax.random.fold_in(keys[8], 2), own, number, COARSE_DEV, N_COL, 2, 2 * CAP, 1))(interp_dest_keys, interp_dest_turns).reshape((COARSE, 2))
    interp_local = touch_ends(jax.random.randint(keys[9], (COARSE, 2), 0, COARSE_DEV), jax.random.fold_in(keys[9], 1), 0, COARSE_DEV - 1).astype(jnp.int32)
    interp_weight = jnp.clip(0.2 + 0.8 * jax.random.uniform(keys[10], (2, FINE), jnp.float32) ** shard_levels(keys[10], (2, FINE), ((1, 64),), -0.2, 0.2), 0.2, 1.0)
    return {"increment": increment, "ensemble": ensemble, "climate": climate, "restrict_dest": restrict_dest, "restrict_local": restrict_local, "restrict_weight": restrict_weight, "conv_blocks": conv_blocks, "neighbours": neighbours, "interp_dest": interp_dest, "interp_local": interp_local, "interp_weight": interp_weight}


def apply_once(state, ensemble, climate, restrict_dest, restrict_local, restrict_weight, conv_blocks, neighbours, interp_dest, interp_local, interp_weight):
    restrict_node = (restrict_dest[:, 0] * COARSE_DEV + restrict_local).astype(jnp.int32)
    interp_node = (interp_dest * COARSE_DEV + interp_local).astype(jnp.int32)
    weighted = state * restrict_weight[None, :]
    tile_weights = interp_weight.reshape(2, COARSE, TILE)
    conv_float = conv_blocks.astype(jnp.float32)

    def member_term(running, member):
        product = member.astype(jnp.float32) * weighted
        partial_value = jnp.sum(product.reshape(LEVELS, COARSE, TILE), axis=2)
        coarse = jax.ops.segment_sum(partial_value.T, restrict_node, num_segments=COARSE)
        coarse = coarse.astype(jnp.bfloat16).astype(jnp.float32)
        blocks = coarse.reshape(BLOCKS, CBLK, LEVELS)
        picked = blocks[neighbours]
        convolved = jnp.einsum("bkij,bkjl->bil", conv_float, picked, precision=lax.Precision.HIGHEST)
        node_values = convolved.reshape(COARSE, LEVELS).astype(jnp.bfloat16).astype(jnp.float32)
        values = node_values[interp_node]
        first_term = values[:, 0, :].T[:, :, None] * tile_weights[0][None, :, :]
        second_term = values[:, 1, :].T[:, :, None] * tile_weights[1][None, :, :]
        interp = (first_term + second_term).reshape(LEVELS, FINE)
        return running + member.astype(jnp.float32) * interp, None

    running, unused = lax.scan(member_term, jnp.zeros((LEVELS, FINE), jnp.float32), ensemble)
    return climate * state + running / (MEMBERS - 1)


def reference(increment, ensemble, climate, restrict_dest, restrict_local, restrict_weight, conv_blocks, neighbours, interp_dest, interp_local, interp_weight):
    once_applied = apply_once(increment, ensemble, climate, restrict_dest, restrict_local, restrict_weight, conv_blocks, neighbours, interp_dest, interp_local, interp_weight)
    twice_applied = apply_once(once_applied, ensemble, climate, restrict_dest, restrict_local, restrict_weight, conv_blocks, neighbours, interp_dest, interp_local, interp_weight)
    return once_applied, twice_applied
```

```python
import functools

import jax
import jax.numpy as jnp
from jax import lax
from jax.experimental import pallas as pl
from jax.experimental.pallas import tpu as pltpu
from jax.sharding import PartitionSpec as P

TILE = 64
CHUNK = 1024
F32 = jnp.float32
BF16 = jnp.bfloat16
MESH = pl.DeviceIdType.MESH


def iota(shape, dim):
    return lax.broadcasted_iota(jnp.int32, shape, dim)


def dot(a, b):
    return jnp.dot(a, b, preferred_element_type=F32)


def dot_tn(a, b):
    return lax.dot_general(a, b, (((0,), (0,)), ((), ())), preferred_element_type=F32)


def ones_where(mask):
    return jnp.where(mask, 1.0, 0.0).astype(BF16)


def kernel(
    cfg,
    neigh_ref,
    inc_ref,
    ens_hbm,
    clim_hbm,
    rd_ref,
    rl_ref,
    rw_ref,
    conv_hbm,
    id_ref,
    il_ref,
    iw_ref,
    once_hbm,
    twice_hbm,
    ens_ref,
    clim_ref,
    conv_ref,
    once_ref,
    twice_ref,
    sum_ref,
    spread_ref,
    pack_ref,
    unpack_ref,
    gather_ref,
    choose_ref,
    partial_ref,
    value_ref,
    a1_send,
    a1_recv,
    ext_first,
    ext_second,
    a2_send,
    a2_recv,
    rs_send,
    rs_recv,
    own_ref,
    ag_send,
    ag_recv,
    in_sem,
    out_sem,
    a1_ssem,
    a1_rsem,
    halo_ssem,
    halo_rsem,
    a2_ssem,
    a2_rsem,
    rs_ssem,
    rs_rsem,
    ag_ssem,
    ag_rsem,
):
    n_col, n_mem, members, levels, fine, cap, scale = cfg
    tiles = fine // TILE
    feature = members * levels
    part = fine // n_mem
    part_tiles = part // TILE
    cap2 = 2 * cap
    slots1 = n_col * cap
    slots2 = n_col * cap2
    me = lax.axis_index("col")
    my_mem = lax.axis_index("mem")
    right = lax.rem(me + 1, n_col)
    left = lax.rem(me + n_col - 1, n_col)

    def ens_load(q):
        cols = pl.ds(q * part, part)
        return pltpu.make_async_copy(
            ens_hbm.at[:, :, cols], ens_ref.at[:, :, cols], in_sem.at[q]
        )

    for q in range(n_mem):
        ens_load(q).start()
    clim_load = pltpu.make_async_copy(clim_hbm, clim_ref, in_sem.at[n_mem])
    clim_load.start()
    conv_load = pltpu.make_async_copy(conv_hbm, conv_ref, in_sem.at[n_mem + 1])
    conv_load.start()

    barrier = pltpu.get_barrier_semaphore()

    @pl.loop(1, n_col)
    def _(i):
        pl.semaphore_signal(
            barrier, inc=1, device_id=(my_mem, lax.rem(me + i, n_col)), device_id_type=MESH
        )

    for i in range(1, n_mem):
        pl.semaphore_signal(
            barrier, inc=1, device_id=(lax.rem(my_mem + i, n_mem), me), device_id_type=MESH
        )

    rows = 512

    @pl.loop(0, part // rows)
    def _(c):
        r = iota((rows, 128), 0) + c * rows
        at = pl.ds(pl.multiple_of(c * rows, rows), rows)
        sum_ref[at, :] = ones_where((r >> 6) == iota((rows, 128), 1))

    owner = rd_ref[pl.ds(me, 1), :]
    slot_row = iota((slots1, tiles), 0)
    named = slot_row // cap == owner
    before = dot(
        ones_where(named), ones_where(iota((tiles, tiles), 0) < iota((tiles, tiles), 1))
    )
    pack_ref[...] = ones_where(named & (before == (slot_row % cap).astype(F32)))

    def restrict(state_ref, q):
        base = q * part

        def body(c, acc):
            off = pl.multiple_of(base + c * CHUNK, CHUNK)
            cols = pl.ds(off, CHUNK)
            w = state_ref[:, cols] * rw_ref[:, cols]
            prod = jnp.concatenate(
                [ens_ref[m, :, cols].astype(F32) * w for m in range(members)], axis=0
            ).astype(BF16)
            at = pl.ds(pl.multiple_of(c * CHUNK, CHUNK), CHUNK)
            return acc + dot(prod, sum_ref[at, :])

        acc = lax.fori_loop(0, part // CHUNK, body, jnp.zeros((feature, 128), F32))
        partial_ref[q] = acc.T[:part_tiles].astype(BF16)

    def all_to_all(src, dst, ssem, rsem):
        @pl.loop(1, n_col)
        def _(i):
            peer = lax.rem(me + i, n_col)
            pltpu.make_async_remote_copy(
                src_ref=src.at[peer],
                dst_ref=dst.at[me],
                send_sem=ssem,
                recv_sem=rsem,
                device_id=(my_mem, peer),
                device_id_type=MESH,
            ).start()

        dst[me] = src[me]

    def wait_blocks(ref, sem):
        some = ref.at[pl.ds(0, n_col - 1)]
        pltpu.make_async_copy(some, some, sem).wait()

    def build_unpack():
        spread = ones_where(iota((n_col, slots1), 0) == iota((n_col, slots1), 1) // cap)
        mine = dot_tn(ones_where(rd_ref[...] == me), spread)
        local = dot_tn(rl_ref[...].astype(F32).astype(BF16), spread)
        before = dot(
            ones_where(iota((tiles, tiles), 1) < iota((tiles, tiles), 0)), mine.astype(BF16)
        )
        slot = (iota((tiles, slots1), 1) % cap).astype(F32)
        hit = jnp.where(before == slot, mine, 0.0)
        node = jnp.sum(hit * local, axis=0, keepdims=True)
        filled = jnp.sum(hit, axis=0, keepdims=True)
        node = jnp.where(filled > 0.5, node, -1.0)
        unpack_ref[...] = ones_where(iota((tiles, slots1), 0).astype(F32) == node)

    def build_gather():
        width = 256
        pairs = 2 * tiles
        mask = ones_where(id_ref[...] == me)
        nodes = il_ref[...].astype(F32).astype(BF16)
        lower = ones_where(iota((pairs, pairs), 1) < iota((pairs, pairs), 0))
        for b in range(slots2 // width):
            column = iota((n_col, width), 1) + b * width
            spread = ones_where(iota((n_col, width), 0) == column // cap2)
            mine = dot_tn(mask, spread)
            local = dot_tn(nodes, spread)
            before = dot(lower, mine.astype(BF16))
            slot = ((iota((pairs, width), 1) + b * width) % cap2).astype(F32)
            hit = jnp.where(before == slot, mine, 0.0)
            node = jnp.sum(hit * local, axis=0, keepdims=True)
            filled = jnp.sum(hit, axis=0, keepdims=True)
            node = jnp.where(filled > 0.5, node, -1.0)
            block = jnp.where(iota((tiles, width), 0).astype(F32) == node, 1.0, 0.0)
            gather_ref[pl.ds(b * width, width), :] = block.T.astype(BF16)

    def build_choose():
        width = 256
        pairs = 2 * tiles
        target = id_ref[pl.ds(me, 1), :]
        upper = ones_where(iota((pairs, pairs), 0) < iota((pairs, pairs), 1))
        for b in range(slots2 // width):
            slot_row = iota((width, pairs), 0) + b * width
            named = slot_row // cap2 == target
            before = dot(ones_where(named), upper)
            block = jnp.where(
                named & (before == (slot_row % cap2).astype(F32)), 1.0, 0.0
            )
            choose_ref[:, pl.ds(b * width, width)] = block.T.astype(BF16)

    def build_spread():
        per = part // CHUNK

        @pl.loop(0, n_mem * per)
        def _(i):
            q = i // per
            c = lax.rem(i, per)
            local = pl.ds(pl.multiple_of(c * CHUNK, CHUNK), CHUNK)
            cols = pl.ds(pl.multiple_of(i * CHUNK, CHUNK), CHUNK)
            shape = (part_tiles, CHUNK)
            mask = ((iota(shape, 1) + c * CHUNK) >> 6) == iota(shape, 0)
            for k in range(2):
                spread_ref[q, pl.ds(k * part_tiles, part_tiles), local] = jnp.where(
                    mask, iw_ref[pl.ds(k, 1), cols], 0.0
                ).astype(BF16)

    def member_sum(q, c):
        off = pl.multiple_of(c * CHUNK, CHUNK)
        interp = dot(value_ref[q], spread_ref[q, :, pl.ds(off, CHUNK)])
        cols = pl.ds(pl.multiple_of(q * part + off, CHUNK), CHUNK)
        total = ens_ref[0, :, cols].astype(F32) * interp[0:levels]
        for m in range(1, members):
            total += ens_ref[m, :, cols].astype(F32) * interp[m * levels : (m + 1) * levels]
        return total

    def result_store(ref, hbm, q, sem):
        cols = pl.ds(pl.multiple_of(q * part, part), part)
        return pltpu.make_async_copy(ref.at[:, cols], hbm.at[:, cols], sem)

    for app in range(2):
        state_ref = inc_ref if app == 0 else once_ref
        new_ref, new_hbm = (once_ref, once_hbm) if app == 0 else (twice_ref, twice_hbm)
        if app == 0:
            for q in range(n_mem):
                ens_load(q).wait()
                restrict(state_ref, q)
        outgoing = dot(pack_ref[...], partial_ref[...].reshape(tiles, feature))
        a1_send[app] = outgoing.reshape(n_col, cap, feature).astype(BF16)
        if app == 0:
            pl.semaphore_wait(barrier, n_col - 1 + n_mem - 1)
        all_to_all(a1_send.at[app], a1_recv.at[app], a1_ssem.at[app], a1_rsem.at[app])
        if app == 0:
            build_unpack()
        wait_blocks(a1_recv.at[app], a1_rsem.at[app])
        ext_ref = ext_first if app == 0 else ext_second
        incoming = a1_recv[app].astype(F32).reshape(slots1, feature).astype(BF16)
        coarse = dot(unpack_ref[...], incoming).astype(BF16)
        ext_ref[2:4] = coarse.reshape(2, tiles // 2, feature)
        halos = []
        for side, peer, at in ((0, right, 0), (1, left, 4)):
            halo = pltpu.make_async_remote_copy(
                src_ref=ext_ref.at[pl.ds(2, 2)],
                dst_ref=ext_ref.at[pl.ds(at, 2)],
                send_sem=halo_ssem.at[app, side],
                recv_sem=halo_rsem.at[app, side],
                device_id=(my_mem, peer),
                device_id_type=MESH,
            )
            halo.start()
            halos.append(halo)
        if app == 0:
            build_gather()
            conv_load.wait()
        for halo in halos:
            halo.wait_recv()
        nodes = []
        for b in range(2):
            total = None
            for k in range(4):
                block = lax.rem(
                    neigh_ref[b, k] - (me - 1) * 2 + 4 * n_col, 2 * n_col
                )
                term = dot(conv_ref[b, k], ext_ref[jnp.minimum(block, 5)])
                total = term if total is None else total + term
            nodes.append(total.astype(BF16))
        replies = dot(gather_ref[...], jnp.concatenate(nodes, axis=0))
        a2_send[app] = replies.astype(BF16).reshape(n_col, cap2, feature)
        all_to_all(a2_send.at[app], a2_recv.at[app], a2_ssem.at[app], a2_rsem.at[app])
        if app == 0:
            build_choose()
            build_spread()
            clim_load.wait()
        wait_blocks(a2_recv.at[app], a2_rsem.at[app])
        answers = a2_recv[app].reshape(slots2, feature)
        fetched = dot(choose_ref[...], answers)
        for q in range(n_mem):
            at = q * 2 * part_tiles
            value_ref[q] = fetched[at : at + 2 * part_tiles].T.astype(BF16)

        scatters = []
        for i in (2, 1, 3):
            q = lax.rem(my_mem + i, n_mem)

            @pl.loop(0, part // CHUNK)
            def _(c, i=i, q=q):
                at = pl.ds(pl.multiple_of(c * CHUNK, CHUNK), CHUNK)
                rs_send[app, i - 1, :, at] = member_sum(q, c).astype(BF16)

            copy = pltpu.make_async_remote_copy(
                src_ref=rs_send.at[app, i - 1],
                dst_ref=rs_recv.at[app, i - 1],
                send_sem=rs_ssem.at[app, i - 1],
                recv_sem=rs_rsem.at[app, i - 1],
                device_id=(q, me),
                device_id_type=MESH,
            )
            copy.start()
            scatters.append(copy)

        @pl.loop(0, part // CHUNK)
        def _(c):
            at = pl.ds(pl.multiple_of(c * CHUNK, CHUNK), CHUNK)
            own_ref[:, at] = member_sum(my_mem, c)

        for copy in scatters:
            copy.wait_recv()
        total = own_ref[...]
        for i in range(n_mem - 1):
            total += rs_recv[app, i].astype(F32)
        ag_send[app] = total.astype(BF16)
        gathers = {}
        for i in (2, 1, 3):
            copy = pltpu.make_async_remote_copy(
                src_ref=ag_send.at[app],
                dst_ref=ag_recv.at[app, i - 1],
                send_sem=ag_ssem.at[app, i - 1],
                recv_sem=ag_rsem.at[app, i - 1],
                device_id=(lax.rem(my_mem + i, n_mem), me),
                device_id_type=MESH,
            )
            copy.start()
            gathers[i] = copy
        for i in (0, 1, 3, 2):
            q = lax.rem(my_mem + n_mem - i, n_mem)
            if i:
                gathers[i].wait_recv()
                summed = ag_recv[app, i - 1]
            else:
                summed = ag_send[app]
            cols = pl.ds(pl.multiple_of(q * part, part), part)
            new_ref[:, cols] = (
                clim_ref[:, cols] * state_ref[:, cols] + summed.astype(F32) * scale
            )
            result_store(new_ref, new_hbm, q, out_sem.at[app, i]).start()
            if app == 0:
                restrict(new_ref, q)
        for copy in scatters:
            copy.wait_send()
        for copy in gathers.values():
            copy.wait_send()
        for halo in halos:
            halo.wait_send()

    for app in range(2):
        wait_blocks(a1_send.at[app], a1_ssem.at[app])
        wait_blocks(a2_send.at[app], a2_ssem.at[app])
        new_ref, new_hbm = (once_ref, once_hbm) if app == 0 else (twice_ref, twice_hbm)
        for i in range(n_mem):
            q = lax.rem(my_mem + n_mem - i, n_mem)
            result_store(new_ref, new_hbm, q, out_sem.at[app, i]).wait()


def per_device(
    increment,
    ensemble,
    climate,
    restrict_dest,
    restrict_local,
    restrict_weight,
    conv_blocks,
    neighbours,
    interp_dest,
    interp_local,
    interp_weight,
):
    n_col = lax.axis_size("col")
    n_mem = lax.axis_size("mem")
    members, levels, fine = ensemble.shape
    tiles = fine // TILE
    part = fine // n_mem
    part_tiles = part // TILE
    feature = members * levels
    cap = max(2, 2 * tiles // n_col)
    scale = 1.0 / (members * n_mem - 1)
    cfg = (n_col, n_mem, members, levels, fine, cap, scale)

    def pairs(a):
        a = a.reshape(n_col, n_mem, part_tiles, 2)
        return a.transpose(0, 1, 3, 2).reshape(n_col, 2 * tiles)

    vmem = pl.BlockSpec(memory_space=pltpu.VMEM)
    smem = pl.BlockSpec(memory_space=pltpu.SMEM)
    hbm = pl.BlockSpec(memory_space=pl.ANY)
    dma = pltpu.SemaphoreType.DMA
    result = jax.ShapeDtypeStruct((levels, fine), F32)
    return pl.pallas_call(
        functools.partial(kernel, cfg),
        out_shape=(result, result),
        in_specs=[smem, vmem, hbm, hbm, vmem, vmem, vmem, hbm, vmem, vmem, vmem],
        out_specs=(hbm, hbm),
        scratch_shapes=[
            pltpu.VMEM((members, levels, fine), BF16),
            pltpu.VMEM((levels, fine), F32),
            pltpu.VMEM(conv_blocks.shape, BF16),
            pltpu.VMEM((levels, fine), F32),
            pltpu.VMEM((levels, fine), F32),
            pltpu.VMEM((part, 128), BF16),
            pltpu.VMEM((n_mem, 2 * part_tiles, part), BF16),
            pltpu.VMEM((n_col * cap, tiles), BF16),
            pltpu.VMEM((tiles, n_col * cap), BF16),
            pltpu.VMEM((n_col * 2 * cap, tiles), BF16),
            pltpu.VMEM((2 * tiles, n_col * 2 * cap), BF16),
            pltpu.VMEM((n_mem, part_tiles, feature), BF16),
            pltpu.VMEM((n_mem, feature, 2 * part_tiles), BF16),
            pltpu.VMEM((2, n_col, cap, feature), BF16),
            pltpu.VMEM((2, n_col, cap, feature), BF16),
            pltpu.VMEM((6, tiles // 2, feature), BF16),
            pltpu.VMEM((6, tiles // 2, feature), BF16),
            pltpu.VMEM((2, n_col, 2 * cap, feature), BF16),
            pltpu.VMEM((2, n_col, 2 * cap, feature), BF16),
            pltpu.VMEM((2, n_mem - 1, levels, part), BF16),
            pltpu.VMEM((2, n_mem - 1, levels, part), BF16),
            pltpu.VMEM((levels, part), F32),
            pltpu.VMEM((2, levels, part), BF16),
            pltpu.VMEM((2, n_mem - 1, levels, part), BF16),
            dma((n_mem + 2,)),
            dma((2, n_mem)),
            dma((2,)),
            dma((2,)),
            dma((2, 2)),
            dma((2, 2)),
            dma((2,)),
            dma((2,)),
            dma((2, n_mem - 1)),
            dma((2, n_mem - 1)),
            dma((2, n_mem - 1)),
            dma((2, n_mem - 1)),
        ],
        compiler_params=pltpu.CompilerParams(
            collective_id=0, has_side_effects=True, vmem_limit_bytes=48 * 1024 * 1024
        ),
        name="covariance_twice",
    )(
        neighbours,
        increment,
        ensemble,
        climate,
        restrict_dest.reshape(n_col, tiles),
        restrict_local.reshape(n_col, tiles),
        restrict_weight.reshape(1, fine),
        conv_blocks,
        pairs(interp_dest),
        pairs(interp_local),
        interp_weight,
    )


def solution(mesh):
    in_specs = (
        P(None, "col"),
        P("mem", None, "col"),
        P(None, "col"),
        P(),
        P(),
        P("col"),
        P("col", None, None, None),
        P("col", None),
        P(),
        P(),
        P(None, "col"),
    )
    out_specs = (P(None, "col"), P(None, "col"))
    return jax.shard_map(
        per_device, mesh=mesh, in_specs=in_specs, out_specs=out_specs, check_vma=False
    )
```

```python
import functools

import jax
import jax.numpy as jnp
from jax import lax
from jax.experimental import pallas as pl
from jax.experimental.pallas import tpu as pltpu
from jax.sharding import PartitionSpec as P

TILE = 64
CHUNK = 1024
LAYER = 8
F32 = jnp.float32
BF16 = jnp.bfloat16
MESH = pl.DeviceIdType.MESH


def iota(shape, dim):
    return lax.broadcasted_iota(jnp.int32, shape, dim)


def dot(a, b):
    return jnp.dot(a, b, preferred_element_type=F32)


def dot_tn(a, b):
    return lax.dot_general(a, b, (((0,), (0,)), ((), ())), preferred_element_type=F32)


def ones_where(mask):
    return jnp.where(mask, 1.0, 0.0).astype(BF16)


def kernel(
    cfg,
    neigh_ref,
    inc_hbm,
    ens_hbm,
    clim_hbm,
    rd_hbm,
    rl_hbm,
    rw_hbm,
    conv_hbm,
    id_hbm,
    il_hbm,
    iw_hbm,
    result_ref,
    inc_ref,
    ens_ref,
    clim_ref,
    rd_ref,
    rl_ref,
    rw_ref,
    conv_ref,
    id_ref,
    il_ref,
    iw_ref,
    once_ref,
    sum_ref,
    spread_ref,
    pack_ref,
    unpack_ref,
    gather_ref,
    choose_ref,
    partial_ref,
    value_ref,
    a1_send,
    a1_recv,
    ext_first,
    ext_second,
    a2_send,
    a2_recv,
    rs_send,
    rs_recv,
    own_ref,
    ag_send,
    ag_recv,
    ens_sem,
    in_sem,
    a1_ssem,
    a1_rsem,
    halo_ssem,
    halo_rsem,
    a2_ssem,
    a2_rsem,
    rs_ssem,
    rs_rsem,
    ag_ssem,
    ag_rsem,
):
    n_col, n_mem, members, levels, fine, cap, scale = cfg
    tiles = fine // TILE
    feature = members * levels
    part = fine // n_mem
    part_tiles = part // TILE
    cap2 = 2 * cap
    slots1 = n_col * cap
    slots2 = n_col * cap2
    me = lax.axis_index("col")
    my_mem = lax.axis_index("mem")
    right = lax.rem(me + 1, n_col)
    left = lax.rem(me + n_col - 1, n_col)

    layers = n_col // LAYER
    my_layer = me // LAYER
    my_place = lax.rem(me, LAYER)
    far_first = sorted(range(layers), key=lambda dz: -min(dz, layers - dz))

    barrier = pltpu.get_barrier_semaphore()
    for dz in far_first:

        @pl.loop(0 if dz else 1, LAYER)
        def _(i, dz=dz):
            peer = lax.rem(my_layer + dz, layers) * LAYER + lax.rem(my_place + i, LAYER)
            pl.semaphore_signal(
                barrier, inc=1, device_id=(my_mem, peer), device_id_type=MESH
            )

    for i in range(1, n_mem):
        pl.semaphore_signal(
            barrier, inc=1, device_id=(lax.rem(my_mem + i, n_mem), me), device_id_type=MESH
        )

    def ens_load(q):
        cols = pl.ds(q * part, part)
        return pltpu.make_async_copy(
            ens_hbm.at[:, :, cols], ens_ref.at[:, :, cols], ens_sem.at[q]
        )

    loads = [
        pltpu.make_async_copy(src, dst, in_sem.at[i])
        for i, (src, dst) in enumerate(
            (
                (rd_hbm, rd_ref),
                (rw_hbm, rw_ref),
                (inc_hbm, inc_ref),
                (rl_hbm, rl_ref),
                (id_hbm, id_ref),
                (il_hbm, il_ref),
                (conv_hbm, conv_ref),
                (iw_hbm, iw_ref),
                (clim_hbm, clim_ref),
            )
        )
    ]
    for load in loads[:3]:
        load.start()
    for q in range(n_mem):
        ens_load(q).start()
    for load in loads[3:]:
        load.start()

    rows = 512

    @pl.loop(0, part // rows)
    def _(c):
        r = iota((rows, 128), 0) + c * rows
        at = pl.ds(pl.multiple_of(c * rows, rows), rows)
        sum_ref[at, :] = ones_where((r >> 6) == iota((rows, 128), 1))

    half = tiles // 2
    loads[0].wait()
    owner = jnp.concatenate(
        [rd_ref[pl.ds(2 * me, 1), :], rd_ref[pl.ds(2 * me + 1, 1), :]], axis=1
    )
    slot_row = iota((slots1, tiles), 0)
    named = slot_row // cap == owner
    before = dot(
        ones_where(named), ones_where(iota((tiles, tiles), 0) < iota((tiles, tiles), 1))
    )
    pack_ref[...] = ones_where(named & (before == (slot_row % cap).astype(F32)))

    def restrict(state_ref, q):
        base = q * part

        def body(c, acc):
            off = pl.multiple_of(base + c * CHUNK, CHUNK)
            cols = pl.ds(off, CHUNK)
            w = state_ref[:, cols] * rw_ref[:, cols]
            prod = jnp.concatenate(
                [ens_ref[m, :, cols].astype(F32) * w for m in range(members)], axis=0
            ).astype(BF16)
            at = pl.ds(pl.multiple_of(c * CHUNK, CHUNK), CHUNK)
            return acc + dot(prod, sum_ref[at, :])

        acc = lax.fori_loop(0, part // CHUNK, body, jnp.zeros((feature, 128), F32))
        partial_ref[q] = acc.T[:part_tiles].astype(BF16)

    def all_to_all(block, src, dst, ssem, rsem):
        for dz in far_first:
            layer = lax.rem(my_layer + dz, layers)
            src[pl.ds(layer * LAYER, LAYER)] = block(layer)

            def send(i, carry, dz=dz, layer=layer):
                peer = layer * LAYER + lax.rem(my_place + 4 + i, LAYER)
                pltpu.make_async_remote_copy(
                    src_ref=src.at[peer],
                    dst_ref=dst.at[me],
                    send_sem=ssem,
                    recv_sem=rsem,
                    device_id=(my_mem, peer),
                    device_id_type=MESH,
                ).start()
                return carry

            if dz:
                lax.fori_loop(0, LAYER, send, 0, unroll=True)
            else:
                lax.fori_loop(0, 4, send, 0, unroll=True)
                lax.fori_loop(5, LAYER, send, 0, unroll=True)
        dst[me] = src[me]

    def wait_blocks(ref, sem):
        some = ref.at[pl.ds(0, n_col - 1)]
        pltpu.make_async_copy(some, some, sem).wait()

    def nodes_of(mask, local, group, groups, width, start, size, many):
        def halves(values):
            found = []
            for g in group:
                column = iota((values.shape[0], width), 1) + start
                spread = ones_where(
                    iota((values.shape[0], width), 0) == column // size * groups + g
                )
                found.append(dot_tn(values, spread))
            return jnp.concatenate(found, axis=0)

        mine = halves(mask)
        names = halves(local)
        lower = ones_where(iota((many, many), 1) < iota((many, many), 0))
        before = dot(lower, mine.astype(BF16))
        slot = ((iota((many, width), 1) + start) % size).astype(F32)
        hit = jnp.where(before == slot, mine, 0.0)
        node = jnp.sum(hit * names, axis=0, keepdims=True)
        filled = jnp.sum(hit, axis=0, keepdims=True)
        node = jnp.where(filled > 0.5, node, -1.0)
        return jnp.where(iota((tiles, width), 0).astype(F32) == node, 1.0, 0.0)

    def build_unpack():
        loads[3].wait()
        unpack_ref[...] = nodes_of(
            ones_where(rd_ref[...] == me),
            rl_ref[...].astype(F32).astype(BF16),
            (0, 1),
            2,
            slots1,
            0,
            cap,
            tiles,
        ).astype(BF16)

    def build_gather():
        width = 256
        loads[4].wait()
        loads[5].wait()
        mask = ones_where(id_ref[...] == me)
        local = il_ref[...].astype(F32).astype(BF16)
        for b in range(slots2 // width):
            block = nodes_of(
                mask, local, (0, 2, 1, 3), 4, width, b * width, cap2, 2 * tiles
            )
            gather_ref[pl.ds(b * width, width), :] = block.T.astype(BF16)

    def build_choose():
        width = 256
        pairs = 2 * tiles
        target = jnp.concatenate(
            [id_ref[pl.ds(4 * me + g, 1), :] for g in (0, 2, 1, 3)], axis=1
        )
        upper = ones_where(iota((pairs, pairs), 0) < iota((pairs, pairs), 1))
        for b in range(slots2 // width):
            slot_row = iota((width, pairs), 0) + b * width
            named = slot_row // cap2 == target
            before = dot(ones_where(named), upper)
            block = jnp.where(
                named & (before == (slot_row % cap2).astype(F32)), 1.0, 0.0
            )
            choose_ref[:, pl.ds(b * width, width)] = block.T.astype(BF16)

    def build_spread():
        per = part // CHUNK

        @pl.loop(0, n_mem * per)
        def _(i):
            q = i // per
            c = lax.rem(i, per)
            local = pl.ds(pl.multiple_of(c * CHUNK, CHUNK), CHUNK)
            cols = pl.ds(pl.multiple_of(i * CHUNK, CHUNK), CHUNK)
            shape = (part_tiles, CHUNK)
            mask = ((iota(shape, 1) + c * CHUNK) >> 6) == iota(shape, 0)
            for k in range(2):
                spread_ref[q, pl.ds(k * part_tiles, part_tiles), local] = jnp.where(
                    mask, iw_ref[pl.ds(k, 1), cols], 0.0
                ).astype(BF16)

    def member_sum(q, c):
        off = pl.multiple_of(c * CHUNK, CHUNK)
        interp = dot(value_ref[q], spread_ref[q, :, pl.ds(off, CHUNK)])
        cols = pl.ds(pl.multiple_of(q * part + off, CHUNK), CHUNK)
        total = ens_ref[0, :, cols].astype(F32) * interp[0:levels]
        for m in range(1, members):
            total += ens_ref[m, :, cols].astype(F32) * interp[m * levels : (m + 1) * levels]
        return total

    for app in range(2):
        state_ref = inc_ref if app == 0 else once_ref
        if app == 0:
            loads[1].wait()
            loads[2].wait()
            for q in range(n_mem):
                ens_load(q).wait()
                restrict(state_ref, q)
        partial = partial_ref[...].reshape(tiles, feature)

        def outgoing(layer):
            rows = LAYER * cap
            at = pl.ds(pl.multiple_of(layer * rows, rows), rows)
            return dot(pack_ref[at, :], partial).reshape(LAYER, cap, feature).astype(BF16)

        if app == 0:
            pl.semaphore_wait(barrier, n_col - 1 + n_mem - 1)
        all_to_all(outgoing, a1_send.at[app], a1_recv.at[app], a1_ssem.at[app], a1_rsem.at[app])
        if app == 0:
            build_unpack()
        wait_blocks(a1_recv.at[app], a1_rsem.at[app])
        ext_ref = ext_first if app == 0 else ext_second
        incoming = a1_recv[app].astype(F32).reshape(slots1, feature).astype(BF16)
        coarse = dot(unpack_ref[...], incoming).astype(BF16)
        ext_ref[2:4] = coarse.reshape(2, tiles // 2, feature)
        halos = []
        for side, peer, at in ((0, right, 0), (1, left, 4)):
            halo = pltpu.make_async_remote_copy(
                src_ref=ext_ref.at[pl.ds(2, 2)],
                dst_ref=ext_ref.at[pl.ds(at, 2)],
                send_sem=halo_ssem.at[app, side],
                recv_sem=halo_rsem.at[app, side],
                device_id=(my_mem, peer),
                device_id_type=MESH,
            )
            halo.start()
            halos.append(halo)
        if app == 0:
            build_gather()
            loads[6].wait()
        for halo in halos:
            halo.wait_recv()
        nodes = []
        for b in range(2):
            total = None
            for k in range(4):
                block = lax.rem(
                    neigh_ref[b, k] - (me - 1) * 2 + 4 * n_col, 2 * n_col
                )
                term = dot(conv_ref[b, k], ext_ref[jnp.minimum(block, 5)])
                total = term if total is None else total + term
            nodes.append(total.astype(BF16))
        nodes = jnp.concatenate(nodes, axis=0)

        def replies(layer):
            rows = LAYER * cap2
            at = pl.ds(pl.multiple_of(layer * rows, rows), rows)
            return dot(gather_ref[at, :], nodes).astype(BF16).reshape(LAYER, cap2, feature)

        all_to_all(replies, a2_send.at[app], a2_recv.at[app], a2_ssem.at[app], a2_rsem.at[app])
        if app == 0:
            build_choose()
            loads[7].wait()
            build_spread()
            loads[8].wait()
        wait_blocks(a2_recv.at[app], a2_rsem.at[app])
        answers = a2_recv[app].reshape(slots2, feature)
        fetched = dot(choose_ref[...], answers)
        for q in range(n_mem):
            at = q * part_tiles
            value_ref[q] = jnp.concatenate(
                [fetched[at : at + part_tiles], fetched[tiles + at : tiles + at + part_tiles]],
                axis=0,
            ).T.astype(BF16)

        scatters = []
        for i in (2, 1, 3):
            q = lax.rem(my_mem + i, n_mem)

            @pl.loop(0, part // CHUNK)
            def _(c, i=i, q=q):
                at = pl.ds(pl.multiple_of(c * CHUNK, CHUNK), CHUNK)
                rs_send[app, i - 1, :, at] = member_sum(q, c).astype(BF16)

            copy = pltpu.make_async_remote_copy(
                src_ref=rs_send.at[app, i - 1],
                dst_ref=rs_recv.at[app, i - 1],
                send_sem=rs_ssem.at[app, i - 1],
                recv_sem=rs_rsem.at[app, i - 1],
                device_id=(q, me),
                device_id_type=MESH,
            )
            copy.start()
            scatters.append(copy)

        @pl.loop(0, part // CHUNK)
        def _(c):
            at = pl.ds(pl.multiple_of(c * CHUNK, CHUNK), CHUNK)
            own_ref[:, at] = member_sum(my_mem, c)

        for copy in scatters:
            copy.wait_recv()
        total = own_ref[...]
        for i in range(n_mem - 1):
            total += rs_recv[app, i].astype(F32)
        ag_send[app] = total.astype(BF16)
        gathers = {}
        for i in (2, 1, 3):
            copy = pltpu.make_async_remote_copy(
                src_ref=ag_send.at[app],
                dst_ref=ag_recv.at[app, i - 1],
                send_sem=ag_ssem.at[app, i - 1],
                recv_sem=ag_rsem.at[app, i - 1],
                device_id=(lax.rem(my_mem + i, n_mem), me),
                device_id_type=MESH,
            )
            copy.start()
            gathers[i] = copy
        for i in (0, 1, 3, 2):
            q = lax.rem(my_mem + n_mem - i, n_mem)
            if i:
                gathers[i].wait_recv()
                summed = ag_recv[app, i - 1]
            else:
                summed = ag_send[app]
            cols = pl.ds(pl.multiple_of(q * part, part), part)
            result_ref[app, :, cols] = summed
            if app == 0:
                once_ref[:, cols] = (
                    clim_ref[:, cols] * inc_ref[:, cols] + summed.astype(F32) * scale
                )
                restrict(once_ref, q)
        for copy in scatters:
            copy.wait_send()
        for copy in gathers.values():
            copy.wait_send()
        for halo in halos:
            halo.wait_send()

    for app in range(2):
        wait_blocks(a1_send.at[app], a1_ssem.at[app])
        wait_blocks(a2_send.at[app], a2_ssem.at[app])


def per_device(
    increment,
    ensemble,
    climate,
    restrict_dest,
    restrict_local,
    restrict_weight,
    conv_blocks,
    neighbours,
    interp_dest,
    interp_local,
    interp_weight,
):
    n_col = lax.axis_size("col")
    n_mem = lax.axis_size("mem")
    members, levels, fine = ensemble.shape
    tiles = fine // TILE
    part = fine // n_mem
    part_tiles = part // TILE
    feature = members * levels
    cap = max(2, 2 * tiles // n_col)
    scale = 1.0 / (members * n_mem - 1)
    cfg = (n_col, n_mem, members, levels, fine, cap, scale)

    blocks = n_col * tiles // 128

    def pairs(a):
        return a.T.reshape(2, blocks, 128).transpose(1, 0, 2).reshape(2 * blocks, 128)

    vmem = pl.BlockSpec(memory_space=pltpu.VMEM)
    smem = pl.BlockSpec(memory_space=pltpu.SMEM)
    hbm = pl.BlockSpec(memory_space=pl.ANY)
    dma = pltpu.SemaphoreType.DMA
    sums = pl.pallas_call(
        functools.partial(kernel, cfg),
        out_shape=jax.ShapeDtypeStruct((2, levels, fine), BF16),
        in_specs=[smem] + [hbm] * 10,
        out_specs=vmem,
        scratch_shapes=[
            pltpu.VMEM((levels, fine), F32),
            pltpu.VMEM((members, levels, fine), BF16),
            pltpu.VMEM((levels, fine), F32),
            pltpu.VMEM((blocks, 128), jnp.int32),
            pltpu.VMEM((blocks, 128), jnp.int32),
            pltpu.VMEM((1, fine), F32),
            pltpu.VMEM(conv_blocks.shape, BF16),
            pltpu.VMEM((2 * blocks, 128), jnp.int32),
            pltpu.VMEM((2 * blocks, 128), jnp.int32),
            pltpu.VMEM((2, fine), F32),
            pltpu.VMEM((levels, fine), F32),
            pltpu.VMEM((part, 128), BF16),
            pltpu.VMEM((n_mem, 2 * part_tiles, part), BF16),
            pltpu.VMEM((n_col * cap, tiles), BF16),
            pltpu.VMEM((tiles, n_col * cap), BF16),
            pltpu.VMEM((n_col * 2 * cap, tiles), BF16),
            pltpu.VMEM((2 * tiles, n_col * 2 * cap), BF16),
            pltpu.VMEM((n_mem, part_tiles, feature), BF16),
            pltpu.VMEM((n_mem, feature, 2 * part_tiles), BF16),
            pltpu.VMEM((2, n_col, cap, feature), BF16),
            pltpu.VMEM((2, n_col, cap, feature), BF16),
            pltpu.VMEM((6, tiles // 2, feature), BF16),
            pltpu.VMEM((6, tiles // 2, feature), BF16),
            pltpu.VMEM((2, n_col, 2 * cap, feature), BF16),
            pltpu.VMEM((2, n_col, 2 * cap, feature), BF16),
            pltpu.VMEM((2, n_mem - 1, levels, part), BF16),
            pltpu.VMEM((2, n_mem - 1, levels, part), BF16),
            pltpu.VMEM((levels, part), F32),
            pltpu.VMEM((2, levels, part), BF16),
            pltpu.VMEM((2, n_mem - 1, levels, part), BF16),
            dma((n_mem,)),
            dma((9,)),
            dma((2,)),
            dma((2,)),
            dma((2, 2)),
            dma((2, 2)),
            dma((2,)),
            dma((2,)),
            dma((2, n_mem - 1)),
            dma((2, n_mem - 1)),
            dma((2, n_mem - 1)),
            dma((2, n_mem - 1)),
        ],
        compiler_params=pltpu.CompilerParams(
            collective_id=0, has_side_effects=True, vmem_limit_bytes=60 * 1024 * 1024
        ),
        name="covariance_twice",
    )(
        neighbours,
        increment,
        ensemble,
        climate,
        restrict_dest.reshape(blocks, 128),
        restrict_local.reshape(blocks, 128),
        restrict_weight.reshape(1, fine),
        conv_blocks,
        pairs(interp_dest),
        pairs(interp_local),
        interp_weight,
    )
    once = climate * increment + sums[0].astype(F32) * scale
    twice = climate * once + sums[1].astype(F32) * scale
    return once, twice


def solution(mesh):
    in_specs = (
        P(None, "col"),
        P("mem", None, "col"),
        P(None, "col"),
        P(),
        P(),
        P("col"),
        P("col", None, None, None),
        P("col", None),
        P(),
        P(),
        P(None, "col"),
    )
    out_specs = (P(None, "col"), P(None, "col"))
    return jax.shard_map(
        per_device, mesh=mesh, in_specs=in_specs, out_specs=out_specs, check_vma=False
    )
```

```python
import functools

import jax
import jax.numpy as jnp
from jax import lax
from jax.experimental import pallas as pl
from jax.experimental.pallas import tpu as pltpu
from jax.sharding import PartitionSpec as P

TILE = 64
CHUNK = 1024
LAYER = 8
F32 = jnp.float32
BF16 = jnp.bfloat16
MESH = pl.DeviceIdType.MESH


def iota(shape, dim):
    return lax.broadcasted_iota(jnp.int32, shape, dim)


def dot(a, b):
    return jnp.dot(a, b, preferred_element_type=F32)


def dot_tn(a, b):
    return lax.dot_general(a, b, (((0,), (0,)), ((), ())), preferred_element_type=F32)


def dot_nt(a, b):
    return lax.dot_general(a, b, (((1,), (1,)), ((), ())), preferred_element_type=F32)


def ones_where(mask):
    return jnp.where(mask, 1.0, 0.0).astype(BF16)


def kernel(
    cfg,
    neigh_ref,
    inc_hbm,
    ens_hbm,
    clim_hbm,
    rd_hbm,
    rl_hbm,
    rw_hbm,
    conv_hbm,
    id_hbm,
    il_hbm,
    iw_hbm,
    once_hbm,
    twice_hbm,
    inc_ref,
    ens_ref,
    clim_ref,
    rd_ref,
    rl_ref,
    rw_ref,
    conv_ref,
    id_ref,
    il_ref,
    iw_ref,
    once_ref,
    twice_ref,
    sum_ref,
    spread_ref,
    pack_ref,
    unpack_ref,
    gather_ref,
    choose_ref,
    partial_ref,
    value_ref,
    a1_send,
    a1_recv,
    ext_first,
    ext_second,
    a2_send,
    a2_recv,
    rs_send,
    rs_recv,
    own_ref,
    ag_send,
    ag_recv,
    ens_sem,
    in_sem,
    out_sem,
    a1_ssem,
    a1_rsem,
    halo_ssem,
    halo_rsem,
    a2_ssem,
    a2_rsem,
    rs_ssem,
    rs_rsem,
    ag_ssem,
    ag_rsem,
):
    n_col, n_mem, members, levels, fine, cap, scale = cfg
    tiles = fine // TILE
    feature = members * levels
    part = fine // n_mem
    part_tiles = part // TILE
    cap2 = 2 * cap
    slots1 = n_col * cap
    slots2 = n_col * cap2
    me = lax.axis_index("col")
    my_mem = lax.axis_index("mem")
    right = lax.rem(me + 1, n_col)
    left = lax.rem(me + n_col - 1, n_col)

    layers = n_col // LAYER
    my_layer = me // LAYER
    my_place = lax.rem(me, LAYER)
    far_first = sorted(range(layers), key=lambda dz: -min(dz, layers - dz))

    barrier = pltpu.get_barrier_semaphore()
    for dz in far_first:

        @pl.loop(0 if dz else 1, LAYER)
        def _(i, dz=dz):
            peer = lax.rem(my_layer + dz, layers) * LAYER + lax.rem(my_place + i, LAYER)
            pl.semaphore_signal(
                barrier, inc=1, device_id=(my_mem, peer), device_id_type=MESH
            )

    for i in range(1, n_mem):
        pl.semaphore_signal(
            barrier, inc=1, device_id=(lax.rem(my_mem + i, n_mem), me), device_id_type=MESH
        )

    def ens_load(q):
        cols = pl.ds(q * part, part)
        return pltpu.make_async_copy(
            ens_hbm.at[:, :, cols], ens_ref.at[:, :, cols], ens_sem.at[q]
        )

    loads = [
        pltpu.make_async_copy(src, dst, in_sem.at[i])
        for i, (src, dst) in enumerate(
            (
                (rd_hbm, rd_ref),
                (rw_hbm, rw_ref),
                (inc_hbm, inc_ref),
                (rl_hbm, rl_ref),
                (id_hbm, id_ref),
                (il_hbm, il_ref),
                (conv_hbm, conv_ref),
                (iw_hbm, iw_ref),
                (clim_hbm, clim_ref),
            )
        )
    ]
    for load in loads[:3]:
        load.start()
    for q in range(n_mem):
        ens_load(q).start()
    for load in loads[3:]:
        load.start()

    chunk_tiles = CHUNK // TILE
    per = part // CHUNK
    sum_ref[...] = ones_where(
        (iota((chunk_tiles, CHUNK), 1) >> 6) == iota((chunk_tiles, CHUNK), 0)
    )

    half = tiles // 2
    loads[0].wait()
    owner = jnp.concatenate(
        [rd_ref[pl.ds(2 * me, 1), :], rd_ref[pl.ds(2 * me + 1, 1), :]], axis=1
    )
    slot_row = iota((slots1, tiles), 0)
    named = slot_row // cap == owner
    before = dot(
        ones_where(named), ones_where(iota((tiles, tiles), 0) < iota((tiles, tiles), 1))
    )
    pack_ref[...] = ones_where(named & (before == (slot_row % cap).astype(F32)))

    def columns(chunk):
        return pl.ds(pl.multiple_of(chunk * CHUNK, CHUNK), CHUNK)

    def restrict(state, chunk):
        cols = columns(chunk)
        w = state * rw_ref[:, cols]
        prod = jnp.concatenate(
            [ens_ref[m, :, cols].astype(F32) * w for m in range(members)], axis=0
        ).astype(BF16)
        partial_ref[chunk] = dot_nt(sum_ref[...], prod).astype(BF16)

    def all_to_all(block, src, dst, ssem, rsem):
        for dz in far_first:
            layer = lax.rem(my_layer + dz, layers)
            src[pl.ds(layer * LAYER, LAYER)] = block(layer)

            def send(i, carry, dz=dz, layer=layer):
                peer = layer * LAYER + lax.rem(my_place + 4 + i, LAYER)
                pltpu.make_async_remote_copy(
                    src_ref=src.at[peer],
                    dst_ref=dst.at[me],
                    send_sem=ssem,
                    recv_sem=rsem,
                    device_id=(my_mem, peer),
                    device_id_type=MESH,
                ).start()
                return carry

            if dz:
                lax.fori_loop(0, LAYER, send, 0, unroll=True)
            else:
                lax.fori_loop(0, 4, send, 0, unroll=True)
                lax.fori_loop(5, LAYER, send, 0, unroll=True)
        dst[me] = src[me]

    def wait_blocks(ref, sem):
        some = ref.at[pl.ds(0, n_col - 1)]
        pltpu.make_async_copy(some, some, sem).wait()

    def nodes_of(mask, local, group, groups, width, start, size, many):
        def halves(values):
            found = []
            for g in group:
                column = iota((values.shape[0], width), 1) + start
                spread = ones_where(
                    iota((values.shape[0], width), 0) == column // size * groups + g
                )
                found.append(dot_tn(values, spread))
            return jnp.concatenate(found, axis=0)

        mine = halves(mask)
        names = halves(local)
        lower = ones_where(iota((many, many), 1) < iota((many, many), 0))
        before = dot(lower, mine.astype(BF16))
        slot = ((iota((many, width), 1) + start) % size).astype(F32)
        hit = jnp.where(before == slot, mine, 0.0)
        node = jnp.sum(hit * names, axis=0, keepdims=True)
        filled = jnp.sum(hit, axis=0, keepdims=True)
        node = jnp.where(filled > 0.5, node, -1.0)
        return jnp.where(iota((tiles, width), 0).astype(F32) == node, 1.0, 0.0)

    def build_unpack():
        loads[3].wait()
        unpack_ref[...] = nodes_of(
            ones_where(rd_ref[...] == me),
            rl_ref[...].astype(F32).astype(BF16),
            (0, 1),
            2,
            slots1,
            0,
            cap,
            tiles,
        ).astype(BF16)

    def build_gather():
        width = 256
        loads[4].wait()
        loads[5].wait()
        mask = ones_where(id_ref[...] == me)
        local = il_ref[...].astype(F32).astype(BF16)
        for b in range(slots2 // width):
            block = nodes_of(
                mask, local, (0, 2, 1, 3), 4, width, b * width, cap2, 2 * tiles
            )
            gather_ref[pl.ds(b * width, width), :] = block.T.astype(BF16)

    def build_choose():
        width = 256
        pairs = 2 * tiles
        target = jnp.concatenate(
            [id_ref[pl.ds(4 * me + g, 1), :] for g in (0, 2, 1, 3)], axis=1
        )
        upper = ones_where(iota((pairs, pairs), 0) < iota((pairs, pairs), 1))
        for b in range(slots2 // width):
            slot_row = iota((width, pairs), 0) + b * width
            named = slot_row // cap2 == target
            before = dot(ones_where(named), upper)
            block = jnp.where(
                named & (before == (slot_row % cap2).astype(F32)), 1.0, 0.0
            )
            choose_ref[:, pl.ds(b * width, width)] = block.T.astype(BF16)

    def build_spread():
        @pl.loop(0, n_mem * per)
        def _(i):
            q = i // per
            c = lax.rem(i, per)
            shape = (part_tiles, CHUNK)
            mask = ((iota(shape, 1) + c * CHUNK) >> 6) == iota(shape, 0)
            for k in range(2):
                spread_ref[q, pl.ds(k * part_tiles, part_tiles), columns(c)] = jnp.where(
                    mask, iw_ref[pl.ds(k, 1), columns(i)], 0.0
                ).astype(BF16)

    def member_sum(q, c):
        interp = dot(value_ref[q], spread_ref[q, :, columns(c)])
        cols = columns(q * per + c)
        total = ens_ref[0, :, cols].astype(F32) * interp[0:levels]
        for m in range(1, members):
            total += ens_ref[m, :, cols].astype(F32) * interp[m * levels : (m + 1) * levels]
        return total

    def wait_all(ref, sem):
        pltpu.make_async_copy(ref, ref, sem).wait()

    for app in range(2):
        old_ref, new_ref, new_hbm = (
            (inc_ref, once_ref, once_hbm) if app == 0 else (once_ref, twice_ref, twice_hbm)
        )
        if app == 0:
            loads[1].wait()
            loads[2].wait()
            for q in range(n_mem):
                ens_load(q).wait()

                def first(c, carry, q=q):
                    chunk = q * per + c
                    restrict(inc_ref[:, columns(chunk)], chunk)
                    return carry

                lax.fori_loop(0, per, first, 0, unroll=2)
        partial = partial_ref[...].reshape(tiles, feature)

        def outgoing(layer):
            rows = LAYER * cap
            at = pl.ds(pl.multiple_of(layer * rows, rows), rows)
            return dot(pack_ref[at, :], partial).reshape(LAYER, cap, feature).astype(BF16)

        if app == 0:
            pl.semaphore_wait(barrier, n_col - 1 + n_mem - 1)
        all_to_all(outgoing, a1_send.at[app], a1_recv.at[app], a1_ssem.at[app], a1_rsem.at[app])
        if app == 0:
            build_unpack()
        wait_blocks(a1_recv.at[app], a1_rsem.at[app])
        ext_ref = ext_first if app == 0 else ext_second
        incoming = a1_recv[app].astype(F32).reshape(slots1, feature).astype(BF16)
        coarse = dot(unpack_ref[...], incoming).astype(BF16)
        ext_ref[2:4] = coarse.reshape(2, tiles // 2, feature)
        halos = []
        for side, peer, at in ((0, right, 0), (1, left, 4)):
            halo = pltpu.make_async_remote_copy(
                src_ref=ext_ref.at[pl.ds(2, 2)],
                dst_ref=ext_ref.at[pl.ds(at, 2)],
                send_sem=halo_ssem.at[app, side],
                recv_sem=halo_rsem.at[app, side],
                device_id=(my_mem, peer),
                device_id_type=MESH,
            )
            halo.start()
            halos.append(halo)
        if app == 0:
            build_gather()
            loads[6].wait()
        for halo in halos:
            halo.wait_recv()
        nodes = []
        for b in range(2):
            total = None
            for k in range(4):
                block = lax.rem(
                    neigh_ref[b, k] - (me - 1) * 2 + 4 * n_col, 2 * n_col
                )
                term = dot(conv_ref[b, k], ext_ref[jnp.minimum(block, 5)])
                total = term if total is None else total + term
            nodes.append(total.astype(BF16))
        nodes = jnp.concatenate(nodes, axis=0)

        def replies(layer):
            rows = LAYER * cap2
            at = pl.ds(pl.multiple_of(layer * rows, rows), rows)
            return dot(gather_ref[at, :], nodes).astype(BF16).reshape(LAYER, cap2, feature)

        all_to_all(replies, a2_send.at[app], a2_recv.at[app], a2_ssem.at[app], a2_rsem.at[app])
        if app == 0:
            build_choose()
            loads[7].wait()
            build_spread()
            loads[8].wait()
        wait_blocks(a2_recv.at[app], a2_rsem.at[app])
        answers = a2_recv[app].reshape(slots2, feature)
        fetched = dot(choose_ref[...], answers)
        for q in range(n_mem):
            at = q * part_tiles
            value_ref[q] = jnp.concatenate(
                [fetched[at : at + part_tiles], fetched[tiles + at : tiles + at + part_tiles]],
                axis=0,
            ).T.astype(BF16)

        @pl.loop(0, per)
        def _(c):
            pieces = []
            for i in (2, 1, 3):
                pieces.append((i, member_sum(lax.rem(my_mem + i, n_mem), c)))
            for i, piece in pieces:
                rs_send[app, c, i - 1] = piece.astype(BF16)
                pltpu.make_async_remote_copy(
                    src_ref=rs_send.at[app, c, i - 1],
                    dst_ref=rs_recv.at[app, c, i - 1],
                    send_sem=rs_ssem.at[app],
                    recv_sem=rs_rsem.at[app, c],
                    device_id=(lax.rem(my_mem + i, n_mem), me),
                    device_id_type=MESH,
                ).start()

        @pl.loop(0, per)
        def _(c):
            own_ref[c] = member_sum(my_mem, c)

        @pl.loop(0, per)
        def _(c):
            wait_all(rs_recv.at[app, c], rs_rsem.at[app, c])
            total = own_ref[c]
            for i in range(n_mem - 1):
                total += rs_recv[app, c, i].astype(F32)
            ag_send[app, c] = total.astype(BF16)
            for i in (2, 1, 3):
                pltpu.make_async_remote_copy(
                    src_ref=ag_send.at[app, c],
                    dst_ref=ag_recv.at[app, c, i - 1],
                    send_sem=ag_ssem.at[app],
                    recv_sem=ag_rsem.at[app, c],
                    device_id=(lax.rem(my_mem + i, n_mem), me),
                    device_id_type=MESH,
                ).start()

        def finish(q, c, summed):
            chunk = q * per + c
            cols = columns(chunk)
            state = clim_ref[:, cols] * old_ref[:, cols] + summed.astype(F32) * scale
            new_ref[:, cols] = state
            pltpu.make_async_copy(
                new_ref.at[:, cols], new_hbm.at[:, cols], out_sem.at[app]
            ).start()
            if app == 0:
                restrict(state, chunk)

        def finish_own(c, carry):
            finish(my_mem, c, ag_send[app, c])
            return carry

        lax.fori_loop(0, per, finish_own, 0, unroll=2)

        @pl.loop(0, per)
        def _(c):
            wait_all(ag_recv.at[app, c], ag_rsem.at[app, c])
            for i in (1, 3, 2):
                finish(lax.rem(my_mem + n_mem - i, n_mem), c, ag_recv[app, c, i - 1])

        wait_all(rs_send.at[app], rs_ssem.at[app])
        wait_all(ag_recv.at[app], ag_ssem.at[app])
        for halo in halos:
            halo.wait_send()

    for app in range(2):
        wait_blocks(a1_send.at[app], a1_ssem.at[app])
        wait_blocks(a2_send.at[app], a2_ssem.at[app])
        wait_all((once_ref, twice_ref)[app], out_sem.at[app])


def per_device(
    increment,
    ensemble,
    climate,
    restrict_dest,
    restrict_local,
    restrict_weight,
    conv_blocks,
    neighbours,
    interp_dest,
    interp_local,
    interp_weight,
):
    n_col = lax.axis_size("col")
    n_mem = lax.axis_size("mem")
    members, levels, fine = ensemble.shape
    tiles = fine // TILE
    part = fine // n_mem
    part_tiles = part // TILE
    per = part // CHUNK
    feature = members * levels
    cap = max(2, 2 * tiles // n_col)
    scale = 1.0 / (members * n_mem - 1)
    cfg = (n_col, n_mem, members, levels, fine, cap, scale)

    blocks = n_col * tiles // 128

    def pairs(a):
        return a.T.reshape(2, blocks, 128).transpose(1, 0, 2).reshape(2 * blocks, 128)

    smem = pl.BlockSpec(memory_space=pltpu.SMEM)
    hbm = pl.BlockSpec(memory_space=pl.ANY)
    dma = pltpu.SemaphoreType.DMA
    result = jax.ShapeDtypeStruct((levels, fine), F32)
    return pl.pallas_call(
        functools.partial(kernel, cfg),
        out_shape=(result, result),
        in_specs=[smem] + [hbm] * 10,
        out_specs=(hbm, hbm),
        scratch_shapes=[
            pltpu.VMEM((levels, fine), F32),
            pltpu.VMEM((members, levels, fine), BF16),
            pltpu.VMEM((levels, fine), F32),
            pltpu.VMEM((blocks, 128), jnp.int32),
            pltpu.VMEM((blocks, 128), jnp.int32),
            pltpu.VMEM((1, fine), F32),
            pltpu.VMEM(conv_blocks.shape, BF16),
            pltpu.VMEM((2 * blocks, 128), jnp.int32),
            pltpu.VMEM((2 * blocks, 128), jnp.int32),
            pltpu.VMEM((2, fine), F32),
            pltpu.VMEM((levels, fine), F32),
            pltpu.VMEM((levels, fine), F32),
            pltpu.VMEM((CHUNK // TILE, CHUNK), BF16),
            pltpu.VMEM((n_mem, 2 * part_tiles, part), BF16),
            pltpu.VMEM((n_col * cap, tiles), BF16),
            pltpu.VMEM((tiles, n_col * cap), BF16),
            pltpu.VMEM((n_col * 2 * cap, tiles), BF16),
            pltpu.VMEM((2 * tiles, n_col * 2 * cap), BF16),
            pltpu.VMEM((fine // CHUNK, CHUNK // TILE, feature), BF16),
            pltpu.VMEM((n_mem, feature, 2 * part_tiles), BF16),
            pltpu.VMEM((2, n_col, cap, feature), BF16),
            pltpu.VMEM((2, n_col, cap, feature), BF16),
            pltpu.VMEM((6, tiles // 2, feature), BF16),
            pltpu.VMEM((6, tiles // 2, feature), BF16),
            pltpu.VMEM((2, n_col, 2 * cap, feature), BF16),
            pltpu.VMEM((2, n_col, 2 * cap, feature), BF16),
            pltpu.VMEM((2, per, n_mem - 1, levels, CHUNK), BF16),
            pltpu.VMEM((2, per, n_mem - 1, levels, CHUNK), BF16),
            pltpu.VMEM((per, levels, CHUNK), F32),
            pltpu.VMEM((2, per, levels, CHUNK), BF16),
            pltpu.VMEM((2, per, n_mem - 1, levels, CHUNK), BF16),
            dma((n_mem,)),
            dma((9,)),
            dma((2,)),
            dma((2,)),
            dma((2,)),
            dma((2, 2)),
            dma((2, 2)),
            dma((2,)),
            dma((2,)),
            dma((2,)),
            dma((2, per)),
            dma((2,)),
            dma((2, per)),
        ],
        compiler_params=pltpu.CompilerParams(
            collective_id=0, has_side_effects=True, vmem_limit_bytes=60 * 1024 * 1024
        ),
        name="covariance_twice",
    )(
        neighbours,
        increment,
        ensemble,
        climate,
        restrict_dest.reshape(blocks, 128),
        restrict_local.reshape(blocks, 128),
        restrict_weight.reshape(1, fine),
        conv_blocks,
        pairs(interp_dest),
        pairs(interp_local),
        interp_weight,
    )


def solution(mesh):
    in_specs = (
        P(None, "col"),
        P("mem", None, "col"),
        P(None, "col"),
        P(),
        P(),
        P("col"),
        P("col", None, None, None),
        P("col", None),
        P(),
        P(),
        P(None, "col"),
    )
    out_specs = (P(None, "col"), P(None, "col"))
    return jax.shard_map(
        per_device, mesh=mesh, in_specs=in_specs, out_specs=out_specs, check_vma=False
    )
```

```python
import functools

import jax
import jax.numpy as jnp
from jax import lax
from jax.experimental import pallas as pl
from jax.experimental.pallas import tpu as pltpu
from jax.sharding import PartitionSpec as P

TILE = 64
CHUNK = 1024
LAYER = 8
F32 = jnp.float32
BF16 = jnp.bfloat16
MESH = pl.DeviceIdType.MESH


def iota(shape, dim):
    return lax.broadcasted_iota(jnp.int32, shape, dim)


def dot(a, b):
    return jnp.dot(a, b, preferred_element_type=F32)


def dot_tn(a, b):
    return lax.dot_general(a, b, (((0,), (0,)), ((), ())), preferred_element_type=F32)


def dot_nt(a, b):
    return lax.dot_general(a, b, (((1,), (1,)), ((), ())), preferred_element_type=F32)


def ones_where(mask):
    return jnp.where(mask, 1.0, 0.0).astype(BF16)


def kernel(
    cfg,
    neigh_ref,
    inc_hbm,
    ens_hbm,
    clim_hbm,
    rd_hbm,
    rl_hbm,
    rw_hbm,
    conv_hbm,
    id_hbm,
    il_hbm,
    iw_hbm,
    once_hbm,
    twice_hbm,
    inc_ref,
    ens_ref,
    clim_ref,
    rd_ref,
    rl_ref,
    rw_ref,
    conv_ref,
    id_ref,
    il_ref,
    iw_ref,
    once_ref,
    twice_ref,
    sum_ref,
    spread_ref,
    pack_ref,
    unpack_ref,
    gather_ref,
    choose_ref,
    partial_ref,
    value_ref,
    a1_send,
    a1_recv,
    ext_first,
    ext_second,
    a2_send,
    a2_recv,
    rs_send,
    rs_recv,
    own_ref,
    ag_send,
    ag_recv,
    ens_sem,
    in_sem,
    out_sem,
    a1_ssem,
    a1_rsem,
    halo_ssem,
    halo_rsem,
    a2_ssem,
    a2_rsem,
    rs_ssem,
    rs_rsem,
    ag_ssem,
    ag_rsem,
):
    n_col, n_mem, members, levels, fine, cap, scale = cfg
    tiles = fine // TILE
    feature = members * levels
    part = fine // n_mem
    part_tiles = part // TILE
    cap2 = 2 * cap
    slots1 = n_col * cap
    slots2 = n_col * cap2
    me = lax.axis_index("col")
    my_mem = lax.axis_index("mem")
    right = lax.rem(me + 1, n_col)
    left = lax.rem(me + n_col - 1, n_col)

    layers = n_col // LAYER
    my_layer = me // LAYER
    my_place = lax.rem(me, LAYER)
    far_first = sorted(range(layers), key=lambda dz: -min(dz, layers - dz))

    barrier = pltpu.get_barrier_semaphore()
    for dz in far_first:

        @pl.loop(0 if dz else 1, LAYER)
        def _(i, dz=dz):
            peer = lax.rem(my_layer + dz, layers) * LAYER + lax.rem(my_place + i, LAYER)
            pl.semaphore_signal(
                barrier, inc=1, device_id=(my_mem, peer), device_id_type=MESH
            )

    for i in range(1, n_mem):
        pl.semaphore_signal(
            barrier, inc=1, device_id=(lax.rem(my_mem + i, n_mem), me), device_id_type=MESH
        )

    def ens_load(q):
        cols = pl.ds(q * part, part)
        return pltpu.make_async_copy(
            ens_hbm.at[:, :, cols], ens_ref.at[:, :, cols], ens_sem.at[q]
        )

    loads = [
        pltpu.make_async_copy(src, dst, in_sem.at[i])
        for i, (src, dst) in enumerate(
            (
                (rd_hbm, rd_ref),
                (rw_hbm, rw_ref),
                (inc_hbm, inc_ref),
                (rl_hbm, rl_ref),
                (id_hbm, id_ref),
                (il_hbm, il_ref),
                (conv_hbm, conv_ref),
                (iw_hbm, iw_ref),
                (clim_hbm, clim_ref),
            )
        )
    ]
    for load in loads[:3]:
        load.start()
    for q in range(n_mem):
        ens_load(q).start()
    for load in loads[3:]:
        load.start()

    chunk_tiles = CHUNK // TILE
    per = part // CHUNK
    sum_ref[...] = ones_where(
        (iota((chunk_tiles, CHUNK), 1) >> 6) == iota((chunk_tiles, CHUNK), 0)
    )

    half = tiles // 2
    loads[0].wait()
    owner = jnp.concatenate(
        [rd_ref[pl.ds(2 * me, 1), :], rd_ref[pl.ds(2 * me + 1, 1), :]], axis=1
    )
    slot_row = iota((slots1, tiles), 0)
    named = slot_row // cap == owner
    before = dot(
        ones_where(named), ones_where(iota((tiles, tiles), 0) < iota((tiles, tiles), 1))
    )
    pack_ref[...] = ones_where(named & (before == (slot_row % cap).astype(F32)))

    def columns(chunk):
        return pl.ds(pl.multiple_of(chunk * CHUNK, CHUNK), CHUNK)

    def restrict(state, chunk):
        cols = columns(chunk)
        w = state * rw_ref[:, cols]
        prod = jnp.concatenate(
            [ens_ref[m, :, cols].astype(F32) * w for m in range(members)], axis=0
        ).astype(BF16)
        partial_ref[chunk] = dot_nt(sum_ref[...], prod).astype(BF16)

    def all_to_all(block, src, dst, ssem, rsem):
        for dz in far_first:
            layer = lax.rem(my_layer + dz, layers)
            src[pl.ds(layer * LAYER, LAYER)] = block(layer)

            def send(i, carry, dz=dz, layer=layer):
                peer = layer * LAYER + lax.rem(my_place + 4 + i, LAYER)
                pltpu.make_async_remote_copy(
                    src_ref=src.at[peer],
                    dst_ref=dst.at[me],
                    send_sem=ssem,
                    recv_sem=rsem.at[my_layer],
                    device_id=(my_mem, peer),
                    device_id_type=MESH,
                ).start()
                return carry

            if dz:
                lax.fori_loop(0, LAYER, send, 0, unroll=True)
            else:
                lax.fori_loop(0, 4, send, 0, unroll=True)
                lax.fori_loop(5, LAYER, send, 0, unroll=True)
        dst[me] = src[me]

    def wait_blocks(ref, sem):
        some = ref.at[pl.ds(0, n_col - 1)]
        pltpu.make_async_copy(some, some, sem).wait()

    def summed_layers(matrix_ref, recv, rsem):
        total = None
        rows = LAYER * recv.shape[1]
        for dz in reversed(far_first):
            layer = lax.rem(my_layer + dz, layers)
            some = recv.at[pl.ds(layer * LAYER, LAYER if dz else LAYER - 1)]
            pltpu.make_async_copy(some, some, rsem.at[layer]).wait()
            blocks = recv[pl.ds(layer * LAYER, LAYER)].astype(F32)
            term = dot(matrix_ref[layer], blocks.reshape(rows, feature).astype(BF16))
            total = term if total is None else total + term
        return total

    def nodes_of(mask, local, group, groups, width, start, size, many):
        def halves(values):
            found = []
            for g in group:
                column = iota((values.shape[0], width), 1) + start
                spread = ones_where(
                    iota((values.shape[0], width), 0) == column // size * groups + g
                )
                found.append(dot_tn(values, spread))
            return jnp.concatenate(found, axis=0)

        mine = halves(mask)
        names = halves(local)
        lower = ones_where(iota((many, many), 1) < iota((many, many), 0))
        before = dot(lower, mine.astype(BF16))
        slot = ((iota((many, width), 1) + start) % size).astype(F32)
        hit = jnp.where(before == slot, mine, 0.0)
        node = jnp.sum(hit * names, axis=0, keepdims=True)
        filled = jnp.sum(hit, axis=0, keepdims=True)
        node = jnp.where(filled > 0.5, node, -1.0)
        return jnp.where(iota((tiles, width), 0).astype(F32) == node, 1.0, 0.0)

    def build_unpack():
        loads[3].wait()
        found = nodes_of(
            ones_where(rd_ref[...] == me),
            rl_ref[...].astype(F32).astype(BF16),
            (0, 1),
            2,
            slots1,
            0,
            cap,
            tiles,
        ).astype(BF16)
        rows = LAYER * cap
        for layer in range(layers):
            unpack_ref[layer] = found[:, layer * rows : (layer + 1) * rows]

    def build_gather():
        width = 256
        loads[4].wait()
        loads[5].wait()
        mask = ones_where(id_ref[...] == me)
        local = il_ref[...].astype(F32).astype(BF16)
        for b in range(slots2 // width):
            block = nodes_of(
                mask, local, (0, 2, 1, 3), 4, width, b * width, cap2, 2 * tiles
            )
            gather_ref[pl.ds(b * width, width), :] = block.T.astype(BF16)

    def build_choose():
        width = LAYER * cap2
        pairs = 2 * tiles
        target = jnp.concatenate(
            [id_ref[pl.ds(4 * me + g, 1), :] for g in (0, 2, 1, 3)], axis=1
        )
        upper = ones_where(iota((pairs, pairs), 0) < iota((pairs, pairs), 1))
        for b in range(slots2 // width):
            slot_row = iota((width, pairs), 0) + b * width
            named = slot_row // cap2 == target
            before = dot(ones_where(named), upper)
            block = jnp.where(
                named & (before == (slot_row % cap2).astype(F32)), 1.0, 0.0
            )
            choose_ref[b] = block.T.astype(BF16)

    def build_spread():
        @pl.loop(0, n_mem * per)
        def _(i):
            q = i // per
            c = lax.rem(i, per)
            shape = (part_tiles, CHUNK)
            mask = ((iota(shape, 1) + c * CHUNK) >> 6) == iota(shape, 0)
            for k in range(2):
                spread_ref[q, pl.ds(k * part_tiles, part_tiles), columns(c)] = jnp.where(
                    mask, iw_ref[pl.ds(k, 1), columns(i)], 0.0
                ).astype(BF16)

    def member_sum(q, c):
        interp = dot(value_ref[q], spread_ref[q, :, columns(c)])
        cols = columns(q * per + c)
        total = ens_ref[0, :, cols].astype(F32) * interp[0:levels]
        for m in range(1, members):
            total += ens_ref[m, :, cols].astype(F32) * interp[m * levels : (m + 1) * levels]
        return total

    def wait_all(ref, sem):
        pltpu.make_async_copy(ref, ref, sem).wait()

    for app in range(2):
        old_ref, new_ref, new_hbm = (
            (inc_ref, once_ref, once_hbm) if app == 0 else (once_ref, twice_ref, twice_hbm)
        )
        if app == 0:
            loads[1].wait()
            loads[2].wait()
            for q in range(n_mem):
                ens_load(q).wait()

                def first(c, carry, q=q):
                    chunk = q * per + c
                    restrict(inc_ref[:, columns(chunk)], chunk)
                    return carry

                lax.fori_loop(0, per, first, 0, unroll=2)
        partial = partial_ref[...].reshape(tiles, feature)

        def outgoing(layer):
            rows = LAYER * cap
            at = pl.ds(pl.multiple_of(layer * rows, rows), rows)
            return dot(pack_ref[at, :], partial).reshape(LAYER, cap, feature).astype(BF16)

        if app == 0:
            pl.semaphore_wait(barrier, n_col - 1 + n_mem - 1)
        all_to_all(outgoing, a1_send.at[app], a1_recv.at[app], a1_ssem.at[app], a1_rsem.at[app])
        if app == 0:
            build_unpack()
        ext_ref = ext_first if app == 0 else ext_second
        coarse = summed_layers(unpack_ref, a1_recv.at[app], a1_rsem.at[app]).astype(BF16)
        ext_ref[2:4] = coarse.reshape(2, tiles // 2, feature)
        halos = []
        for side, peer, at in ((0, right, 0), (1, left, 4)):
            halo = pltpu.make_async_remote_copy(
                src_ref=ext_ref.at[pl.ds(2, 2)],
                dst_ref=ext_ref.at[pl.ds(at, 2)],
                send_sem=halo_ssem.at[app, side],
                recv_sem=halo_rsem.at[app, side],
                device_id=(my_mem, peer),
                device_id_type=MESH,
            )
            halo.start()
            halos.append(halo)
        if app == 0:
            build_gather()
            loads[6].wait()
        for halo in halos:
            halo.wait_recv()
        nodes = []
        for b in range(2):
            picked = []
            for k in range(4):
                block = lax.rem(
                    neigh_ref[b, k] - (me - 1) * 2 + 4 * n_col, 2 * n_col
                )
                picked.append(ext_ref[jnp.minimum(block, 5)])
            blocks = jnp.concatenate([conv_ref[b, k] for k in range(4)], axis=1)
            nodes.append(dot(blocks, jnp.concatenate(picked, axis=0)).astype(BF16))
        nodes = jnp.concatenate(nodes, axis=0)

        def replies(layer):
            rows = LAYER * cap2
            at = pl.ds(pl.multiple_of(layer * rows, rows), rows)
            return dot(gather_ref[at, :], nodes).astype(BF16).reshape(LAYER, cap2, feature)

        all_to_all(replies, a2_send.at[app], a2_recv.at[app], a2_ssem.at[app], a2_rsem.at[app])
        if app == 0:
            build_choose()
            loads[7].wait()
            build_spread()
            loads[8].wait()
        fetched = summed_layers(choose_ref, a2_recv.at[app], a2_rsem.at[app])
        for q in range(n_mem):
            at = q * part_tiles
            value_ref[q] = jnp.concatenate(
                [fetched[at : at + part_tiles], fetched[tiles + at : tiles + at + part_tiles]],
                axis=0,
            ).T.astype(BF16)

        @pl.loop(0, per)
        def _(c):
            pieces = []
            for i in (2, 1, 3):
                pieces.append((i, member_sum(lax.rem(my_mem + i, n_mem), c)))
            for i, piece in pieces:
                rs_send[app, c, i - 1] = piece.astype(BF16)
                pltpu.make_async_remote_copy(
                    src_ref=rs_send.at[app, c, i - 1],
                    dst_ref=rs_recv.at[app, c, i - 1],
                    send_sem=rs_ssem.at[app],
                    recv_sem=rs_rsem.at[app, c],
                    device_id=(lax.rem(my_mem + i, n_mem), me),
                    device_id_type=MESH,
                ).start()

        @pl.loop(0, per)
        def _(c):
            own_ref[c] = member_sum(my_mem, c)

        @pl.loop(0, per)
        def _(c):
            wait_all(rs_recv.at[app, c], rs_rsem.at[app, c])
            total = own_ref[c]
            for i in range(n_mem - 1):
                total += rs_recv[app, c, i].astype(F32)
            ag_send[app, c] = total.astype(BF16)
            for i in (2, 1, 3):
                pltpu.make_async_remote_copy(
                    src_ref=ag_send.at[app, c],
                    dst_ref=ag_recv.at[app, c, i - 1],
                    send_sem=ag_ssem.at[app],
                    recv_sem=ag_rsem.at[app, c],
                    device_id=(lax.rem(my_mem + i, n_mem), me),
                    device_id_type=MESH,
                ).start()

        def finish(q, c, summed):
            chunk = q * per + c
            cols = columns(chunk)
            state = clim_ref[:, cols] * old_ref[:, cols] + summed.astype(F32) * scale
            new_ref[:, cols] = state
            pltpu.make_async_copy(
                new_ref.at[:, cols], new_hbm.at[:, cols], out_sem.at[app]
            ).start()
            if app == 0:
                restrict(state, chunk)

        def finish_own(c, carry):
            finish(my_mem, c, ag_send[app, c])
            return carry

        lax.fori_loop(0, per, finish_own, 0, unroll=2)

        @pl.loop(0, per)
        def _(c):
            wait_all(ag_recv.at[app, c], ag_rsem.at[app, c])
            for i in (1, 3, 2):
                finish(lax.rem(my_mem + n_mem - i, n_mem), c, ag_recv[app, c, i - 1])

        wait_all(rs_send.at[app], rs_ssem.at[app])
        wait_all(ag_recv.at[app], ag_ssem.at[app])
        for halo in halos:
            halo.wait_send()

    for app in range(2):
        wait_blocks(a1_send.at[app], a1_ssem.at[app])
        wait_blocks(a2_send.at[app], a2_ssem.at[app])
        wait_all((once_ref, twice_ref)[app], out_sem.at[app])


def result_kernel(once_in, twice_in, once_out, twice_out, once_ref, twice_ref, sem):
    pieces = 4
    width = once_ref.shape[1] // pieces
    pairs = []
    for k, (src, ref, dst) in enumerate(
        ((once_in, once_ref, once_out), (twice_in, twice_ref, twice_out))
    ):
        for p in range(pieces):
            cols = pl.ds(p * width, width)
            pairs.append(
                (
                    pltpu.make_async_copy(src.at[:, cols], ref.at[:, cols], sem.at[0, k, p]),
                    pltpu.make_async_copy(ref.at[:, cols], dst.at[:, cols], sem.at[1, k, p]),
                )
            )
    for load, _ in pairs:
        load.start()
    for load, store in pairs:
        load.wait()
        store.start()
    for _, store in pairs:
        store.wait()


def per_device(
    increment,
    ensemble,
    climate,
    restrict_dest,
    restrict_local,
    restrict_weight,
    conv_blocks,
    neighbours,
    interp_dest,
    interp_local,
    interp_weight,
):
    n_col = lax.axis_size("col")
    n_mem = lax.axis_size("mem")
    members, levels, fine = ensemble.shape
    tiles = fine // TILE
    part = fine // n_mem
    part_tiles = part // TILE
    per = part // CHUNK
    feature = members * levels
    cap = max(2, 2 * tiles // n_col)
    scale = 1.0 / (members * n_mem - 1)
    cfg = (n_col, n_mem, members, levels, fine, cap, scale)

    blocks = n_col * tiles // 128

    def pairs(a):
        return a.T.reshape(2, blocks, 128).transpose(1, 0, 2).reshape(2 * blocks, 128)

    smem = pl.BlockSpec(memory_space=pltpu.SMEM)
    hbm = pl.BlockSpec(memory_space=pl.ANY)
    dma = pltpu.SemaphoreType.DMA
    result = jax.ShapeDtypeStruct((levels, fine), F32)
    once, twice = pl.pallas_call(
        functools.partial(kernel, cfg),
        out_shape=(result, result),
        in_specs=[smem] + [hbm] * 10,
        out_specs=(hbm, hbm),
        scratch_shapes=[
            pltpu.VMEM((levels, fine), F32),
            pltpu.VMEM((members, levels, fine), BF16),
            pltpu.VMEM((levels, fine), F32),
            pltpu.VMEM((blocks, 128), jnp.int32),
            pltpu.VMEM((blocks, 128), jnp.int32),
            pltpu.VMEM((1, fine), F32),
            pltpu.VMEM(conv_blocks.shape, BF16),
            pltpu.VMEM((2 * blocks, 128), jnp.int32),
            pltpu.VMEM((2 * blocks, 128), jnp.int32),
            pltpu.VMEM((2, fine), F32),
            pltpu.VMEM((levels, fine), F32),
            pltpu.VMEM((levels, fine), F32),
            pltpu.VMEM((CHUNK // TILE, CHUNK), BF16),
            pltpu.VMEM((n_mem, 2 * part_tiles, part), BF16),
            pltpu.VMEM((n_col * cap, tiles), BF16),
            pltpu.VMEM((n_col // LAYER, tiles, LAYER * cap), BF16),
            pltpu.VMEM((n_col * 2 * cap, tiles), BF16),
            pltpu.VMEM((n_col // LAYER, 2 * tiles, LAYER * 2 * cap), BF16),
            pltpu.VMEM((fine // CHUNK, CHUNK // TILE, feature), BF16),
            pltpu.VMEM((n_mem, feature, 2 * part_tiles), BF16),
            pltpu.VMEM((2, n_col, cap, feature), BF16),
            pltpu.VMEM((2, n_col, cap, feature), BF16),
            pltpu.VMEM((6, tiles // 2, feature), BF16),
            pltpu.VMEM((6, tiles // 2, feature), BF16),
            pltpu.VMEM((2, n_col, 2 * cap, feature), BF16),
            pltpu.VMEM((2, n_col, 2 * cap, feature), BF16),
            pltpu.VMEM((2, per, n_mem - 1, levels, CHUNK), BF16),
            pltpu.VMEM((2, per, n_mem - 1, levels, CHUNK), BF16),
            pltpu.VMEM((per, levels, CHUNK), F32),
            pltpu.VMEM((2, per, levels, CHUNK), BF16),
            pltpu.VMEM((2, per, n_mem - 1, levels, CHUNK), BF16),
            dma((n_mem,)),
            dma((9,)),
            dma((2,)),
            dma((2,)),
            dma((2, n_col // LAYER)),
            dma((2, 2)),
            dma((2, 2)),
            dma((2,)),
            dma((2, n_col // LAYER)),
            dma((2,)),
            dma((2, per)),
            dma((2,)),
            dma((2, per)),
        ],
        compiler_params=pltpu.CompilerParams(
            collective_id=0, has_side_effects=True, vmem_limit_bytes=60 * 1024 * 1024
        ),
        name="covariance_twice",
    )(
        neighbours,
        increment,
        ensemble,
        climate,
        restrict_dest.reshape(blocks, 128),
        restrict_local.reshape(blocks, 128),
        restrict_weight.reshape(1, fine),
        conv_blocks,
        pairs(interp_dest),
        pairs(interp_local),
        interp_weight,
    )
    return pl.pallas_call(
        result_kernel,
        out_shape=(result, result),
        in_specs=[hbm, hbm],
        out_specs=(hbm, hbm),
        scratch_shapes=[
            pltpu.VMEM((levels, fine), F32),
            pltpu.VMEM((levels, fine), F32),
            dma((2, 2, 4)),
        ],
        compiler_params=pltpu.CompilerParams(vmem_limit_bytes=60 * 1024 * 1024),
        name="results",
    )(once, twice)


def solution(mesh):
    in_specs = (
        P(None, "col"),
        P("mem", None, "col"),
        P(None, "col"),
        P(),
        P(),
        P("col"),
        P("col", None, None, None),
        P("col", None),
        P(),
        P(),
        P(None, "col"),
    )
    out_specs = (P(None, "col"), P(None, "col"))
    return jax.shard_map(
        per_device, mesh=mesh, in_specs=in_specs, out_specs=out_specs, check_vma=False
    )
```

```python
import functools

import jax
import jax.numpy as jnp
from jax import lax
from jax.experimental import pallas as pl
from jax.experimental.pallas import tpu as pltpu
from jax.sharding import PartitionSpec as P

TILE = 64
CHUNK = 1024
LAYER = 8
F32 = jnp.float32
BF16 = jnp.bfloat16
MESH = pl.DeviceIdType.MESH


def iota(shape, dim):
    return lax.broadcasted_iota(jnp.int32, shape, dim)


def dot(a, b):
    return jnp.dot(a, b, preferred_element_type=F32)


def dot_tn(a, b):
    return lax.dot_general(a, b, (((0,), (0,)), ((), ())), preferred_element_type=F32)


def dot_nt(a, b):
    return lax.dot_general(a, b, (((1,), (1,)), ((), ())), preferred_element_type=F32)


def ones_where(mask):
    return jnp.where(mask, 1.0, 0.0).astype(BF16)


def kernel(
    cfg,
    neigh_ref,
    inc_hbm,
    ens_hbm,
    clim_hbm,
    rd_hbm,
    rl_hbm,
    rw_hbm,
    conv_hbm,
    id_hbm,
    il_hbm,
    iw_hbm,
    once_hbm,
    twice_hbm,
    inc_ref,
    ens_ref,
    clim_ref,
    rd_ref,
    rl_ref,
    rw_ref,
    conv_ref,
    id_ref,
    il_ref,
    iw_ref,
    once_ref,
    twice_ref,
    sum_ref,
    spread_ref,
    pack_ref,
    unpack_ref,
    gather_ref,
    choose_ref,
    partial_ref,
    value_ref,
    a1_send,
    a1_recv,
    ext_first,
    ext_second,
    a2_send,
    a2_recv,
    rs_send,
    rs_recv,
    own_ref,
    ag_send,
    ag_recv,
    ens_sem,
    in_sem,
    out_sem,
    a1_ssem,
    a1_rsem,
    halo_ssem,
    halo_rsem,
    a2_ssem,
    a2_rsem,
    rs_ssem,
    rs_rsem,
    ag_ssem,
    ag_rsem,
):
    n_col, n_mem, members, levels, fine, cap, scale = cfg
    tiles = fine // TILE
    feature = members * levels
    part = fine // n_mem
    part_tiles = part // TILE
    cap2 = 2 * cap
    slots1 = n_col * cap
    slots2 = n_col * cap2
    me = lax.axis_index("col")
    my_mem = lax.axis_index("mem")
    core = lax.rem(me, 2)
    partner = me + 1 - 2 * core

    layers = n_col // LAYER
    my_layer = me // LAYER
    my_place = lax.rem(me, LAYER)
    far_first = sorted(range(layers), key=lambda dz: -min(dz, layers - dz))

    def ens_load(q):
        cols = pl.ds(q * part, part)
        return pltpu.make_async_copy(
            ens_hbm.at[:, :, cols], ens_ref.at[:, :, cols], ens_sem.at[q]
        )

    loads = [
        pltpu.make_async_copy(src, dst, in_sem.at[i])
        for i, (src, dst) in enumerate(
            (
                (rd_hbm, rd_ref),
                (rw_hbm, rw_ref),
                (inc_hbm, inc_ref),
                (rl_hbm, rl_ref),
                (id_hbm, id_ref),
                (il_hbm, il_ref),
                (conv_hbm, conv_ref),
                (iw_hbm, iw_ref),
                (clim_hbm, clim_ref),
            )
        )
    ]
    for load in loads[:3]:
        load.start()
    for q in range(n_mem):
        ens_load(q).start()
    barrier = pltpu.get_barrier_semaphore()
    for dz in far_first:

        @pl.loop(0 if dz else 1, LAYER)
        def _(i, dz=dz):
            peer = lax.rem(my_layer + dz, layers) * LAYER + lax.rem(my_place + i, LAYER)
            pl.semaphore_signal(
                barrier, inc=1, device_id=(my_mem, peer), device_id_type=MESH
            )

    for i in range(1, n_mem):
        pl.semaphore_signal(
            barrier, inc=1, device_id=(lax.rem(my_mem + i, n_mem), me), device_id_type=MESH
        )

    for load in loads[3:]:
        load.start()

    chunk_tiles = CHUNK // TILE
    per = part // CHUNK
    sum_ref[...] = ones_where(
        (iota((chunk_tiles, CHUNK), 1) >> 6) == iota((chunk_tiles, CHUNK), 0)
    )

    half = tiles // 2
    loads[0].wait()
    owner = jnp.concatenate(
        [rd_ref[pl.ds(2 * me, 1), :], rd_ref[pl.ds(2 * me + 1, 1), :]], axis=1
    )
    slot_row = iota((slots1, tiles), 0)
    named = slot_row // cap == owner
    before = dot(
        ones_where(named), ones_where(iota((tiles, tiles), 0) < iota((tiles, tiles), 1))
    )
    pack_ref[...] = ones_where(named & (before == (slot_row % cap).astype(F32)))

    def columns(chunk):
        return pl.ds(pl.multiple_of(chunk * CHUNK, CHUNK), CHUNK)

    def restrict(state, chunk):
        cols = columns(chunk)
        w = state * rw_ref[:, cols]
        prod = jnp.concatenate(
            [ens_ref[m, :, cols].astype(F32) * w for m in range(members)], axis=0
        ).astype(BF16)
        partial_ref[chunk] = dot_nt(sum_ref[...], prod).astype(BF16)

    def all_to_all(ready, source, dst, ssem, rsem):
        for dz in far_first:
            layer = lax.rem(my_layer + dz, layers)
            ready(layer)

            def send(i, carry, dz=dz, layer=layer):
                peer = layer * LAYER + lax.rem(my_place + 4 + i, LAYER)
                pltpu.make_async_remote_copy(
                    src_ref=source(peer),
                    dst_ref=dst.at[me],
                    send_sem=ssem,
                    recv_sem=rsem,
                    device_id=(my_mem, peer),
                    device_id_type=MESH,
                ).start()
                return carry

            if dz:
                lax.fori_loop(0, LAYER, send, 0, unroll=True)
            else:
                lax.fori_loop(0, 4, send, 0, unroll=True)
                lax.fori_loop(5, LAYER, send, 0, unroll=True)

    def wait_blocks(ref, sem):
        some = ref.at[pl.ds(0, n_col - 1)]
        pltpu.make_async_copy(some, some, sem).wait()

    def nodes_of(mask, local, group, groups, width, start, size, many):
        def halves(values):
            found = []
            for g in group:
                column = iota((values.shape[0], width), 1) + start
                spread = ones_where(
                    iota((values.shape[0], width), 0) == column // size * groups + g
                )
                found.append(dot_tn(values, spread))
            return jnp.concatenate(found, axis=0)

        mine = halves(mask)
        names = halves(local)
        lower = ones_where(iota((many, many), 1) < iota((many, many), 0))
        before = dot(lower, mine.astype(BF16))
        slot = ((iota((many, width), 1) + start) % size).astype(F32)
        hit = jnp.where(before == slot, mine, 0.0)
        node = jnp.sum(hit * names, axis=0, keepdims=True)
        filled = jnp.sum(hit, axis=0, keepdims=True)
        node = jnp.where(filled > 0.5, node, -1.0)
        return jnp.where(iota((tiles, width), 0).astype(F32) == node, 1.0, 0.0)

    def build_unpack():
        loads[3].wait()
        local = rl_ref[...].astype(F32).astype(BF16)
        for o in range(2):
            who = lax.rem(me + core + o + n_col - 1, n_col)
            mask = ones_where(rd_ref[...] == who)
            found = nodes_of(mask, local, (0, 1), 2, slots1, 0, cap, tiles)
            unpack_ref[o] = found.astype(BF16)

    def build_gather():
        width = 256
        loads[4].wait()
        loads[5].wait()
        mask = ones_where(id_ref[...] == me)
        local = il_ref[...].astype(F32).astype(BF16)
        for b in range(slots2 // width):
            block = nodes_of(
                mask, local, (0, 2, 1, 3), 4, width, b * width, cap2, 2 * tiles
            )
            gather_ref[pl.ds(b * width, width), :] = block.T.astype(BF16)

    def build_choose():
        width = 256
        pairs = 2 * tiles
        target = jnp.concatenate(
            [id_ref[pl.ds(4 * me + g, 1), :] for g in (0, 2, 1, 3)], axis=1
        )
        upper = ones_where(iota((pairs, pairs), 0) < iota((pairs, pairs), 1))
        for b in range(slots2 // width):
            slot_row = iota((width, pairs), 0) + b * width
            named = slot_row // cap2 == target
            before = dot(ones_where(named), upper)
            block = jnp.where(
                named & (before == (slot_row % cap2).astype(F32)), 1.0, 0.0
            )
            choose_ref[:, pl.ds(b * width, width)] = block.T.astype(BF16)

    def build_spread():
        @pl.loop(0, n_mem * per)
        def _(i):
            q = i // per
            c = lax.rem(i, per)
            shape = (part_tiles, CHUNK)
            mask = ((iota(shape, 1) + c * CHUNK) >> 6) == iota(shape, 0)
            for k in range(2):
                spread_ref[q, pl.ds(k * part_tiles, part_tiles), columns(c)] = jnp.where(
                    mask, iw_ref[pl.ds(k, 1), columns(i)], 0.0
                ).astype(BF16)

    def member_sum(q, c):
        interp = dot(value_ref[q], spread_ref[q, :, columns(c)])
        cols = columns(q * per + c)
        total = ens_ref[0, :, cols].astype(F32) * interp[0:levels]
        for m in range(1, members):
            total += ens_ref[m, :, cols].astype(F32) * interp[m * levels : (m + 1) * levels]
        return total

    def wait_all(ref, sem):
        pltpu.make_async_copy(ref, ref, sem).wait()

    for app in range(2):
        old_ref, new_ref, new_hbm = (
            (inc_ref, once_ref, once_hbm) if app == 0 else (once_ref, twice_ref, twice_hbm)
        )
        if app == 0:
            loads[1].wait()
            loads[2].wait()
            for q in range(n_mem):
                ens_load(q).wait()

                def first(c, carry, q=q):
                    chunk = q * per + c
                    restrict(inc_ref[:, columns(chunk)], chunk)
                    return carry

                lax.fori_loop(0, per, first, 0, unroll=4)
        partial = partial_ref[...].reshape(tiles, feature)

        outgoing = dot(pack_ref[...], partial).reshape(n_col, cap, feature).astype(BF16)
        a1_send[app, pl.ds(1, n_col)] = outgoing
        a1_send[app, 0] = outgoing[n_col - 1]
        a1_send[app, n_col + 1] = outgoing[0]
        if app == 0:
            pl.semaphore_wait(barrier, n_col - 1 + n_mem - 1)

        def two_owners(peer):
            return a1_send.at[app, pl.ds(peer + lax.rem(peer, 2), 2)]

        all_to_all(
            lambda layer: None, two_owners, a1_recv.at[app], a1_ssem.at[app], a1_rsem.at[app]
        )
        a1_recv[app, me] = a1_send[app, pl.ds(me + core, 2)]
        if app == 0:
            build_unpack()
        wait_blocks(a1_recv.at[app], a1_rsem.at[app])
        ext_ref = ext_first if app == 0 else ext_second

        def coarse(o):
            incoming = a1_recv[app, :, o].astype(F32).reshape(slots1, feature)
            values = dot(unpack_ref[o], incoming.astype(BF16)).astype(BF16)
            return values.reshape(2, tiles // 2, feature)

        ext_ref[pl.ds(2, 2)] = coarse(1 - core)
        halo = pltpu.make_async_remote_copy(
            src_ref=ext_ref.at[pl.ds(2, 2)],
            dst_ref=ext_ref.at[pl.ds(4 * core, 2)],
            send_sem=halo_ssem.at[app],
            recv_sem=halo_rsem.at[app],
            device_id=(my_mem, partner),
            device_id_type=MESH,
        )
        halo.start()
        ext_ref[pl.ds(4 * core, 2)] = coarse(core)
        if app == 0:
            build_gather()
            loads[6].wait()
        halo.wait_recv()
        nodes = []
        for b in range(2):
            picked = []
            for k in range(4):
                block = lax.rem(
                    neigh_ref[b, k] - (me - 1) * 2 + 4 * n_col, 2 * n_col
                )
                picked.append(ext_ref[jnp.minimum(block, 5)])
            blocks = jnp.concatenate([conv_ref[b, k] for k in range(4)], axis=1)
            nodes.append(dot(blocks, jnp.concatenate(picked, axis=0)).astype(BF16))
        nodes = jnp.concatenate(nodes, axis=0)

        def replies(layer):
            rows = LAYER * cap2
            at = pl.ds(pl.multiple_of(layer * rows, rows), rows)
            block = dot(gather_ref[at, :], nodes).astype(BF16)
            a2_send[app, pl.ds(layer * LAYER, LAYER)] = block.reshape(LAYER, cap2, feature)

        all_to_all(replies, lambda peer: a2_send.at[app, peer], a2_recv.at[app], a2_ssem.at[app], a2_rsem.at[app])
        a2_recv[app, me] = a2_send[app, me]
        if app == 0:
            build_choose()
            loads[7].wait()
            build_spread()
            loads[8].wait()
        wait_blocks(a2_recv.at[app], a2_rsem.at[app])
        fetched = dot(choose_ref[...], a2_recv[app].reshape(slots2, feature))
        for q in range(n_mem):
            at = q * part_tiles
            value_ref[q] = jnp.concatenate(
                [fetched[at : at + part_tiles], fetched[tiles + at : tiles + at + part_tiles]],
                axis=0,
            ).T.astype(BF16)

        @pl.loop(0, per)
        def _(c):
            pieces = []
            for i in (2, 1, 3):
                pieces.append((i, member_sum(lax.rem(my_mem + i, n_mem), c)))
            for i, piece in pieces:
                rs_send[app, c, i - 1] = piece.astype(BF16)
                pltpu.make_async_remote_copy(
                    src_ref=rs_send.at[app, c, i - 1],
                    dst_ref=rs_recv.at[app, c, i - 1],
                    send_sem=rs_ssem.at[app],
                    recv_sem=rs_rsem.at[app, c],
                    device_id=(lax.rem(my_mem + i, n_mem), me),
                    device_id_type=MESH,
                ).start()

        @pl.loop(0, per)
        def _(c):
            own_ref[c] = member_sum(my_mem, c)

        @pl.loop(0, per)
        def _(c):
            wait_all(rs_recv.at[app, c], rs_rsem.at[app, c])
            total = own_ref[c]
            for i in range(n_mem - 1):
                total += rs_recv[app, c, i].astype(F32)
            ag_send[app, c] = total.astype(BF16)
            for i in (2, 1, 3):
                pltpu.make_async_remote_copy(
                    src_ref=ag_send.at[app, c],
                    dst_ref=ag_recv.at[app, c, i - 1],
                    send_sem=ag_ssem.at[app],
                    recv_sem=ag_rsem.at[app, c],
                    device_id=(lax.rem(my_mem + i, n_mem), me),
                    device_id_type=MESH,
                ).start()

        def finish(q, c, summed):
            chunk = q * per + c
            cols = columns(chunk)
            state = clim_ref[:, cols] * old_ref[:, cols] + summed.astype(F32) * scale
            new_ref[:, cols] = state
            pltpu.make_async_copy(
                new_ref.at[:, cols], new_hbm.at[:, cols], out_sem.at[app]
            ).start()
            if app == 0:
                restrict(state, chunk)

        def finish_own(c, carry):
            finish(my_mem, c, ag_send[app, c])
            return carry

        lax.fori_loop(0, per, finish_own, 0, unroll=2)

        @pl.loop(0, per)
        def _(c):
            wait_all(ag_recv.at[app, c], ag_rsem.at[app, c])
            for i in (1, 3, 2):
                finish(lax.rem(my_mem + n_mem - i, n_mem), c, ag_recv[app, c, i - 1])

        wait_all(rs_send.at[app], rs_ssem.at[app])
        wait_all(ag_recv.at[app], ag_ssem.at[app])
        halo.wait_send()

    for app in range(2):
        wait_blocks(a1_recv.at[app], a1_ssem.at[app])
        wait_blocks(a2_send.at[app], a2_ssem.at[app])
        wait_all((once_ref, twice_ref)[app], out_sem.at[app])


def result_kernel(once_in, twice_in, once_out, twice_out, once_ref, twice_ref, sem):
    pieces = 4
    width = once_ref.shape[1] // pieces
    pairs = []
    for k, (src, ref, dst) in enumerate(
        ((once_in, once_ref, once_out), (twice_in, twice_ref, twice_out))
    ):
        for p in range(pieces):
            cols = pl.ds(p * width, width)
            pairs.append(
                (
                    pltpu.make_async_copy(src.at[:, cols], ref.at[:, cols], sem.at[0, k, p]),
                    pltpu.make_async_copy(ref.at[:, cols], dst.at[:, cols], sem.at[1, k, p]),
                )
            )
    for load, _ in pairs:
        load.start()
    for load, store in pairs:
        load.wait()
        store.start()
    for _, store in pairs:
        store.wait()


def per_device(
    increment,
    ensemble,
    climate,
    restrict_dest,
    restrict_local,
    restrict_weight,
    conv_blocks,
    neighbours,
    interp_dest,
    interp_local,
    interp_weight,
):
    n_col = lax.axis_size("col")
    n_mem = lax.axis_size("mem")
    members, levels, fine = ensemble.shape
    tiles = fine // TILE
    part = fine // n_mem
    part_tiles = part // TILE
    per = part // CHUNK
    feature = members * levels
    cap = max(2, 2 * tiles // n_col)
    scale = 1.0 / (members * n_mem - 1)
    cfg = (n_col, n_mem, members, levels, fine, cap, scale)

    blocks = n_col * tiles // 128

    def pairs(a):
        return a.T.reshape(2, blocks, 128).transpose(1, 0, 2).reshape(2 * blocks, 128)

    smem = pl.BlockSpec(memory_space=pltpu.SMEM)
    hbm = pl.BlockSpec(memory_space=pl.ANY)
    dma = pltpu.SemaphoreType.DMA
    result = jax.ShapeDtypeStruct((levels, fine), F32)
    once, twice = pl.pallas_call(
        functools.partial(kernel, cfg),
        out_shape=(result, result),
        in_specs=[smem] + [hbm] * 10,
        out_specs=(hbm, hbm),
        scratch_shapes=[
            pltpu.VMEM((levels, fine), F32),
            pltpu.VMEM((members, levels, fine), BF16),
            pltpu.VMEM((levels, fine), F32),
            pltpu.VMEM((blocks, 128), jnp.int32),
            pltpu.VMEM((blocks, 128), jnp.int32),
            pltpu.VMEM((1, fine), F32),
            pltpu.VMEM(conv_blocks.shape, BF16),
            pltpu.VMEM((2 * blocks, 128), jnp.int32),
            pltpu.VMEM((2 * blocks, 128), jnp.int32),
            pltpu.VMEM((2, fine), F32),
            pltpu.VMEM((levels, fine), F32),
            pltpu.VMEM((levels, fine), F32),
            pltpu.VMEM((CHUNK // TILE, CHUNK), BF16),
            pltpu.VMEM((n_mem, 2 * part_tiles, part), BF16),
            pltpu.VMEM((n_col * cap, tiles), BF16),
            pltpu.VMEM((2, tiles, n_col * cap), BF16),
            pltpu.VMEM((n_col * 2 * cap, tiles), BF16),
            pltpu.VMEM((2 * tiles, n_col * 2 * cap), BF16),
            pltpu.VMEM((fine // CHUNK, CHUNK // TILE, feature), BF16),
            pltpu.VMEM((n_mem, feature, 2 * part_tiles), BF16),
            pltpu.VMEM((2, n_col + 2, cap, feature), BF16),
            pltpu.VMEM((2, n_col, 2, cap, feature), BF16),
            pltpu.VMEM((6, tiles // 2, feature), BF16),
            pltpu.VMEM((6, tiles // 2, feature), BF16),
            pltpu.VMEM((2, n_col, 2 * cap, feature), BF16),
            pltpu.VMEM((2, n_col, 2 * cap, feature), BF16),
            pltpu.VMEM((2, per, n_mem - 1, levels, CHUNK), BF16),
            pltpu.VMEM((2, per, n_mem - 1, levels, CHUNK), BF16),
            pltpu.VMEM((per, levels, CHUNK), F32),
            pltpu.VMEM((2, per, levels, CHUNK), BF16),
            pltpu.VMEM((2, per, n_mem - 1, levels, CHUNK), BF16),
            dma((n_mem,)),
            dma((9,)),
            dma((2,)),
            dma((2,)),
            dma((2,)),
            dma((2,)),
            dma((2,)),
            dma((2,)),
            dma((2,)),
            dma((2,)),
            dma((2, per)),
            dma((2,)),
            dma((2, per)),
        ],
        compiler_params=pltpu.CompilerParams(
            collective_id=0, has_side_effects=True, vmem_limit_bytes=60 * 1024 * 1024
        ),
        name="covariance_twice",
    )(
        neighbours,
        increment,
        ensemble,
        climate,
        restrict_dest.reshape(blocks, 128),
        restrict_local.reshape(blocks, 128),
        restrict_weight.reshape(1, fine),
        conv_blocks,
        pairs(interp_dest),
        pairs(interp_local),
        interp_weight,
    )
    return pl.pallas_call(
        result_kernel,
        out_shape=(result, result),
        in_specs=[hbm, hbm],
        out_specs=(hbm, hbm),
        scratch_shapes=[
            pltpu.VMEM((levels, fine), F32),
            pltpu.VMEM((levels, fine), F32),
            dma((2, 2, 4)),
        ],
        compiler_params=pltpu.CompilerParams(vmem_limit_bytes=60 * 1024 * 1024),
        name="results",
    )(once, twice)


def solution(mesh):
    in_specs = (
        P(None, "col"),
        P("mem", None, "col"),
        P(None, "col"),
        P(),
        P(),
        P("col"),
        P("col", None, None, None),
        P("col", None),
        P(),
        P(),
        P(None, "col"),
    )
    out_specs = (P(None, "col"), P(None, "col"))
    return jax.shard_map(
        per_device, mesh=mesh, in_specs=in_specs, out_specs=out_specs, check_vma=False
    )
```

```python
import functools

import jax
import jax.numpy as jnp
from jax import lax
from jax.experimental import pallas as pl
from jax.experimental.pallas import tpu as pltpu
from jax.sharding import PartitionSpec as P

TILE = 64
CHUNK = 1024
LAYER = 8
F32 = jnp.float32
BF16 = jnp.bfloat16
MESH = pl.DeviceIdType.MESH


def iota(shape, dim):
    return lax.broadcasted_iota(jnp.int32, shape, dim)


def dot(a, b):
    return jnp.dot(a, b, preferred_element_type=F32)


def dot_tn(a, b):
    return lax.dot_general(a, b, (((0,), (0,)), ((), ())), preferred_element_type=F32)


def dot_nt(a, b):
    return lax.dot_general(a, b, (((1,), (1,)), ((), ())), preferred_element_type=F32)


def ones_where(mask):
    return jnp.where(mask, 1.0, 0.0).astype(BF16)


def kernel(
    cfg,
    neigh_ref,
    inc_hbm,
    ens_hbm,
    clim_hbm,
    rd_hbm,
    rl_hbm,
    rw_hbm,
    conv_hbm,
    id_hbm,
    il_hbm,
    iw_hbm,
    once_hbm,
    twice_hbm,
    inc_ref,
    ens_ref,
    clim_ref,
    rd_ref,
    rl_ref,
    rw_ref,
    conv_ref,
    id_ref,
    il_ref,
    iw_ref,
    once_ref,
    twice_ref,
    sum_ref,
    spread_ref,
    pack_ref,
    unpack_ref,
    gather_ref,
    choose_ref,
    partial_ref,
    value_ref,
    a1_send,
    a1_recv,
    ext_first,
    ext_second,
    a2_send,
    a2_recv,
    rs_send,
    rs_recv,
    own_ref,
    ag_send,
    ag_recv,
    ens_sem,
    in_sem,
    out_sem,
    a1_ssem,
    a1_rsem,
    halo_ssem,
    halo_rsem,
    a2_ssem,
    a2_rsem,
    rs_ssem,
    rs_rsem,
    ag_ssem,
    ag_rsem,
):
    n_col, n_mem, members, levels, fine, cap, scale = cfg
    tiles = fine // TILE
    feature = members * levels
    part = fine // n_mem
    part_tiles = part // TILE
    cap2 = 2 * cap
    slots1 = n_col * cap
    slots2 = n_col * cap2
    me = lax.axis_index("col")
    my_mem = lax.axis_index("mem")
    right = lax.rem(me + 1, n_col)
    left = lax.rem(me + n_col - 1, n_col)

    layers = n_col // LAYER
    my_layer = me // LAYER
    my_place = lax.rem(me, LAYER)
    far_first = sorted(range(layers), key=lambda dz: -min(dz, layers - dz))

    def ens_load(q):
        cols = pl.ds(q * part, part)
        return pltpu.make_async_copy(
            ens_hbm.at[:, :, cols], ens_ref.at[:, :, cols], ens_sem.at[q]
        )

    loads = [
        pltpu.make_async_copy(src, dst, in_sem.at[i])
        for i, (src, dst) in enumerate(
            (
                (rd_hbm, rd_ref),
                (rw_hbm, rw_ref),
                (inc_hbm, inc_ref),
                (rl_hbm, rl_ref),
                (id_hbm, id_ref),
                (il_hbm, il_ref),
                (conv_hbm, conv_ref),
                (iw_hbm, iw_ref),
                (clim_hbm, clim_ref),
            )
        )
    ]
    for load in loads[:3]:
        load.start()
    for q in range(n_mem):
        ens_load(q).start()
    barrier = pltpu.get_barrier_semaphore()
    for dz in far_first:

        @pl.loop(0 if dz else 1, LAYER)
        def _(i, dz=dz):
            peer = lax.rem(my_layer + dz, layers) * LAYER + lax.rem(my_place + i, LAYER)
            pl.semaphore_signal(
                barrier, inc=1, device_id=(my_mem, peer), device_id_type=MESH
            )

    for i in range(1, n_mem):
        pl.semaphore_signal(
            barrier, inc=1, device_id=(lax.rem(my_mem + i, n_mem), me), device_id_type=MESH
        )

    for load in loads[3:]:
        load.start()

    chunk_tiles = CHUNK // TILE
    per = part // CHUNK
    sum_ref[...] = ones_where(
        (iota((chunk_tiles, CHUNK), 1) >> 6) == iota((chunk_tiles, CHUNK), 0)
    )

    half = tiles // 2
    loads[0].wait()
    owner = jnp.concatenate(
        [rd_ref[pl.ds(2 * me, 1), :], rd_ref[pl.ds(2 * me + 1, 1), :]], axis=1
    )
    slot_row = iota((slots1, tiles), 0)
    named = slot_row // cap == owner
    before = dot(
        ones_where(named), ones_where(iota((tiles, tiles), 0) < iota((tiles, tiles), 1))
    )
    pack_ref[...] = ones_where(named & (before == (slot_row % cap).astype(F32)))

    def columns(chunk):
        return pl.ds(pl.multiple_of(chunk * CHUNK, CHUNK), CHUNK)

    def restrict(state, chunk):
        cols = columns(chunk)
        w = state * rw_ref[:, cols]
        prod = jnp.concatenate(
            [ens_ref[m, :, cols].astype(F32) * w for m in range(members)], axis=0
        ).astype(BF16)
        partial_ref[chunk] = dot_nt(sum_ref[...], prod).astype(BF16)

    def all_to_all(block, src, dst, ssem, rsem):
        for dz in far_first:
            layer = lax.rem(my_layer + dz, layers)
            src[pl.ds(layer * LAYER, LAYER)] = block(layer)

            def send(i, carry, dz=dz, layer=layer):
                peer = layer * LAYER + lax.rem(my_place + 4 + i, LAYER)
                pltpu.make_async_remote_copy(
                    src_ref=src.at[peer],
                    dst_ref=dst.at[me],
                    send_sem=ssem,
                    recv_sem=rsem,
                    device_id=(my_mem, peer),
                    device_id_type=MESH,
                ).start()
                return carry

            if dz:
                lax.fori_loop(0, LAYER, send, 0, unroll=True)
            else:
                lax.fori_loop(0, 4, send, 0, unroll=True)
                lax.fori_loop(5, LAYER, send, 0, unroll=True)
        dst[me] = src[me]

    def wait_blocks(ref, sem):
        some = ref.at[pl.ds(0, n_col - 1)]
        pltpu.make_async_copy(some, some, sem).wait()

    def nodes_of(mask, local, group, groups, width, start, size, many):
        def halves(values):
            found = []
            for g in group:
                column = iota((values.shape[0], width), 1) + start
                spread = ones_where(
                    iota((values.shape[0], width), 0) == column // size * groups + g
                )
                found.append(dot_tn(values, spread))
            return jnp.concatenate(found, axis=0)

        mine = halves(mask)
        names = halves(local)
        lower = ones_where(iota((many, many), 1) < iota((many, many), 0))
        before = dot(lower, mine.astype(BF16))
        slot = ((iota((many, width), 1) + start) % size).astype(F32)
        hit = jnp.where(before == slot, mine, 0.0)
        node = jnp.sum(hit * names, axis=0, keepdims=True)
        filled = jnp.sum(hit, axis=0, keepdims=True)
        node = jnp.where(filled > 0.5, node, -1.0)
        return jnp.where(iota((tiles, width), 0).astype(F32) == node, 1.0, 0.0)

    def build_unpack():
        loads[3].wait()
        unpack_ref[...] = nodes_of(
            ones_where(rd_ref[...] == me),
            rl_ref[...].astype(F32).astype(BF16),
            (0, 1),
            2,
            slots1,
            0,
            cap,
            tiles,
        ).astype(BF16)

    def build_gather():
        width = 256
        loads[4].wait()
        loads[5].wait()
        mask = ones_where(id_ref[...] == me)
        local = il_ref[...].astype(F32).astype(BF16)
        for b in range(slots2 // width):
            block = nodes_of(
                mask, local, (0, 2, 1, 3), 4, width, b * width, cap2, 2 * tiles
            )
            gather_ref[pl.ds(b * width, width), :] = block.T.astype(BF16)

    def build_choose():
        width = 256
        pairs = 2 * tiles
        target = jnp.concatenate(
            [id_ref[pl.ds(4 * me + g, 1), :] for g in (0, 2, 1, 3)], axis=1
        )
        upper = ones_where(iota((pairs, pairs), 0) < iota((pairs, pairs), 1))
        for b in range(slots2 // width):
            slot_row = iota((width, pairs), 0) + b * width
            named = slot_row // cap2 == target
            before = dot(ones_where(named), upper)
            block = jnp.where(
                named & (before == (slot_row % cap2).astype(F32)), 1.0, 0.0
            )
            block = block.T.astype(BF16)
            for q in range(n_mem):
                for k in range(2):
                    at = k * tiles + q * part_tiles
                    choose_ref[q, pl.ds(k * part_tiles, part_tiles), pl.ds(b * width, width)] = (
                        block[at : at + part_tiles]
                    )

    def build_spread():
        @pl.loop(0, n_mem * per)
        def _(i):
            q = i // per
            c = lax.rem(i, per)
            shape = (part_tiles, CHUNK)
            mask = ((iota(shape, 1) + c * CHUNK) >> 6) == iota(shape, 0)
            for k in range(2):
                spread_ref[q, pl.ds(k * part_tiles, part_tiles), columns(c)] = jnp.where(
                    mask, iw_ref[pl.ds(k, 1), columns(i)], 0.0
                ).astype(BF16)

    def member_sum(q, c):
        interp = dot(value_ref[q], spread_ref[q, :, columns(c)])
        cols = columns(q * per + c)
        total = ens_ref[0, :, cols].astype(F32) * interp[0:levels]
        for m in range(1, members):
            total += ens_ref[m, :, cols].astype(F32) * interp[m * levels : (m + 1) * levels]
        return total

    def wait_all(ref, sem):
        pltpu.make_async_copy(ref, ref, sem).wait()

    for app in range(2):
        old_ref, new_ref, new_hbm = (
            (inc_ref, once_ref, once_hbm) if app == 0 else (once_ref, twice_ref, twice_hbm)
        )
        if app == 0:
            loads[1].wait()
            loads[2].wait()
            for q in range(n_mem):
                ens_load(q).wait()

                def first(c, carry, q=q):
                    chunk = q * per + c
                    restrict(inc_ref[:, columns(chunk)], chunk)
                    return carry

                lax.fori_loop(0, per, first, 0, unroll=2)
        partial = partial_ref[...].reshape(tiles, feature)

        def outgoing(layer):
            rows = LAYER * cap
            at = pl.ds(pl.multiple_of(layer * rows, rows), rows)
            return dot(pack_ref[at, :], partial).reshape(LAYER, cap, feature).astype(BF16)

        if app == 0:
            pl.semaphore_wait(barrier, n_col - 1 + n_mem - 1)
        all_to_all(outgoing, a1_send.at[app], a1_recv.at[app], a1_ssem.at[app], a1_rsem.at[app])
        if app == 0:
            build_unpack()
        wait_blocks(a1_recv.at[app], a1_rsem.at[app])
        ext_ref = ext_first if app == 0 else ext_second
        incoming = a1_recv[app].astype(F32).reshape(slots1, feature).astype(BF16)
        coarse = dot(unpack_ref[...], incoming).astype(BF16)
        ext_ref[2:4] = coarse.reshape(2, tiles // 2, feature)
        halos = []
        for side, peer, at in ((0, right, 0), (1, left, 4)):
            halo = pltpu.make_async_remote_copy(
                src_ref=ext_ref.at[pl.ds(2, 2)],
                dst_ref=ext_ref.at[pl.ds(at, 2)],
                send_sem=halo_ssem.at[app, side],
                recv_sem=halo_rsem.at[app, side],
                device_id=(my_mem, peer),
                device_id_type=MESH,
            )
            halo.start()
            halos.append(halo)
        if app == 0:
            build_gather()
            loads[6].wait()
        for halo in halos:
            halo.wait_recv()
        nodes = []
        for b in range(2):
            total = None
            for k in range(4):
                block = lax.rem(
                    neigh_ref[b, k] - (me - 1) * 2 + 4 * n_col, 2 * n_col
                )
                term = dot(conv_ref[b, k], ext_ref[jnp.minimum(block, 5)])
                total = term if total is None else total + term
            nodes.append(total.astype(BF16))
        nodes = jnp.concatenate(nodes, axis=0)

        def replies(layer):
            rows = LAYER * cap2
            at = pl.ds(pl.multiple_of(layer * rows, rows), rows)
            return dot(gather_ref[at, :], nodes).astype(BF16).reshape(LAYER, cap2, feature)

        all_to_all(replies, a2_send.at[app], a2_recv.at[app], a2_ssem.at[app], a2_rsem.at[app])
        if app == 0:
            build_choose()
            loads[7].wait()
            build_spread()
            loads[8].wait()
        wait_blocks(a2_recv.at[app], a2_rsem.at[app])
        answers = a2_recv[app].reshape(slots2, feature)

        def fetch(q):
            value_ref[q] = dot(choose_ref[q], answers).T.astype(BF16)

        for i in (2, 1, 3):
            fetch(lax.rem(my_mem + i, n_mem))

        @pl.loop(0, per)
        def _(c):
            pieces = []
            for i in (2, 1, 3):
                pieces.append((i, member_sum(lax.rem(my_mem + i, n_mem), c)))
            for i, piece in pieces:
                rs_send[app, c, i - 1] = piece.astype(BF16)
                pltpu.make_async_remote_copy(
                    src_ref=rs_send.at[app, c, i - 1],
                    dst_ref=rs_recv.at[app, c, i - 1],
                    send_sem=rs_ssem.at[app],
                    recv_sem=rs_rsem.at[app, c],
                    device_id=(lax.rem(my_mem + i, n_mem), me),
                    device_id_type=MESH,
                ).start()

        fetch(my_mem)

        @pl.loop(0, per)
        def _(c):
            own_ref[c] = member_sum(my_mem, c)

        @pl.loop(0, per)
        def _(c):
            wait_all(rs_recv.at[app, c], rs_rsem.at[app, c])
            total = own_ref[c]
            for i in range(n_mem - 1):
                total += rs_recv[app, c, i].astype(F32)
            ag_send[app, c] = total.astype(BF16)
            for i in (2, 1, 3):
                pltpu.make_async_remote_copy(
                    src_ref=ag_send.at[app, c],
                    dst_ref=ag_recv.at[app, c, i - 1],
                    send_sem=ag_ssem.at[app],
                    recv_sem=ag_rsem.at[app, c],
                    device_id=(lax.rem(my_mem + i, n_mem), me),
                    device_id_type=MESH,
                ).start()

        def finish(q, c, summed):
            chunk = q * per + c
            cols = columns(chunk)
            state = clim_ref[:, cols] * old_ref[:, cols] + summed.astype(F32) * scale
            new_ref[:, cols] = state
            pltpu.make_async_copy(
                new_ref.at[:, cols], new_hbm.at[:, cols], out_sem.at[app]
            ).start()
            if app == 0:
                restrict(state, chunk)

        def finish_own(c, carry):
            finish(my_mem, c, ag_send[app, c])
            return carry

        lax.fori_loop(0, per, finish_own, 0, unroll=2)

        @pl.loop(0, per)
        def _(c):
            wait_all(ag_recv.at[app, c], ag_rsem.at[app, c])
            for i in (1, 3, 2):
                finish(lax.rem(my_mem + n_mem - i, n_mem), c, ag_recv[app, c, i - 1])

        wait_all(rs_send.at[app], rs_ssem.at[app])
        wait_all(ag_recv.at[app], ag_ssem.at[app])
        for halo in halos:
            halo.wait_send()

    for app in range(2):
        wait_blocks(a1_send.at[app], a1_ssem.at[app])
        wait_blocks(a2_send.at[app], a2_ssem.at[app])
        wait_all((once_ref, twice_ref)[app], out_sem.at[app])


def result_kernel(once_in, twice_in, once_out, twice_out, once_ref, twice_ref, sem):
    pieces = 4
    width = once_ref.shape[1] // pieces
    pairs = []
    for k, (src, ref, dst) in enumerate(
        ((once_in, once_ref, once_out), (twice_in, twice_ref, twice_out))
    ):
        for p in range(pieces):
            cols = pl.ds(p * width, width)
            pairs.append(
                (
                    pltpu.make_async_copy(src.at[:, cols], ref.at[:, cols], sem.at[0, k, p]),
                    pltpu.make_async_copy(ref.at[:, cols], dst.at[:, cols], sem.at[1, k, p]),
                )
            )
    for load, _ in pairs:
        load.start()
    for load, store in pairs:
        load.wait()
        store.start()
    for _, store in pairs:
        store.wait()


def per_device(
    increment,
    ensemble,
    climate,
    restrict_dest,
    restrict_local,
    restrict_weight,
    conv_blocks,
    neighbours,
    interp_dest,
    interp_local,
    interp_weight,
):
    n_col = lax.axis_size("col")
    n_mem = lax.axis_size("mem")
    members, levels, fine = ensemble.shape
    tiles = fine // TILE
    part = fine // n_mem
    part_tiles = part // TILE
    per = part // CHUNK
    feature = members * levels
    cap = max(2, 2 * tiles // n_col)
    scale = 1.0 / (members * n_mem - 1)
    cfg = (n_col, n_mem, members, levels, fine, cap, scale)

    blocks = n_col * tiles // 128

    def pairs(a):
        return a.T.reshape(2, blocks, 128).transpose(1, 0, 2).reshape(2 * blocks, 128)

    smem = pl.BlockSpec(memory_space=pltpu.SMEM)
    hbm = pl.BlockSpec(memory_space=pl.ANY)
    dma = pltpu.SemaphoreType.DMA
    result = jax.ShapeDtypeStruct((levels, fine), F32)
    once, twice = pl.pallas_call(
        functools.partial(kernel, cfg),
        out_shape=(result, result),
        in_specs=[smem] + [hbm] * 10,
        out_specs=(hbm, hbm),
        scratch_shapes=[
            pltpu.VMEM((levels, fine), F32),
            pltpu.VMEM((members, levels, fine), BF16),
            pltpu.VMEM((levels, fine), F32),
            pltpu.VMEM((blocks, 128), jnp.int32),
            pltpu.VMEM((blocks, 128), jnp.int32),
            pltpu.VMEM((1, fine), F32),
            pltpu.VMEM(conv_blocks.shape, BF16),
            pltpu.VMEM((2 * blocks, 128), jnp.int32),
            pltpu.VMEM((2 * blocks, 128), jnp.int32),
            pltpu.VMEM((2, fine), F32),
            pltpu.VMEM((levels, fine), F32),
            pltpu.VMEM((levels, fine), F32),
            pltpu.VMEM((CHUNK // TILE, CHUNK), BF16),
            pltpu.VMEM((n_mem, 2 * part_tiles, part), BF16),
            pltpu.VMEM((n_col * cap, tiles), BF16),
            pltpu.VMEM((tiles, n_col * cap), BF16),
            pltpu.VMEM((n_col * 2 * cap, tiles), BF16),
            pltpu.VMEM((n_mem, 2 * part_tiles, n_col * 2 * cap), BF16),
            pltpu.VMEM((fine // CHUNK, CHUNK // TILE, feature), BF16),
            pltpu.VMEM((n_mem, feature, 2 * part_tiles), BF16),
            pltpu.VMEM((2, n_col, cap, feature), BF16),
            pltpu.VMEM((2, n_col, cap, feature), BF16),
            pltpu.VMEM((6, tiles // 2, feature), BF16),
            pltpu.VMEM((6, tiles // 2, feature), BF16),
            pltpu.VMEM((2, n_col, 2 * cap, feature), BF16),
            pltpu.VMEM((2, n_col, 2 * cap, feature), BF16),
            pltpu.VMEM((2, per, n_mem - 1, levels, CHUNK), BF16),
            pltpu.VMEM((2, per, n_mem - 1, levels, CHUNK), BF16),
            pltpu.VMEM((per, levels, CHUNK), F32),
            pltpu.VMEM((2, per, levels, CHUNK), BF16),
            pltpu.VMEM((2, per, n_mem - 1, levels, CHUNK), BF16),
            dma((n_mem,)),
            dma((9,)),
            dma((2,)),
            dma((2,)),
            dma((2,)),
            dma((2, 2)),
            dma((2, 2)),
            dma((2,)),
            dma((2,)),
            dma((2,)),
            dma((2, per)),
            dma((2,)),
            dma((2, per)),
        ],
        compiler_params=pltpu.CompilerParams(
            collective_id=0, has_side_effects=True, vmem_limit_bytes=60 * 1024 * 1024
        ),
        name="covariance_twice",
    )(
        neighbours,
        increment,
        ensemble,
        climate,
        restrict_dest.reshape(blocks, 128),
        restrict_local.reshape(blocks, 128),
        restrict_weight.reshape(1, fine),
        conv_blocks,
        pairs(interp_dest),
        pairs(interp_local),
        interp_weight,
    )
    return pl.pallas_call(
        result_kernel,
        out_shape=(result, result),
        in_specs=[hbm, hbm],
        out_specs=(hbm, hbm),
        scratch_shapes=[
            pltpu.VMEM((levels, fine), F32),
            pltpu.VMEM((levels, fine), F32),
            dma((2, 2, 4)),
        ],
        compiler_params=pltpu.CompilerParams(vmem_limit_bytes=60 * 1024 * 1024),
        name="results",
    )(once, twice)


def solution(mesh):
    in_specs = (
        P(None, "col"),
        P("mem", None, "col"),
        P(None, "col"),
        P(),
        P(),
        P("col"),
        P("col", None, None, None),
        P("col", None),
        P(),
        P(),
        P(None, "col"),
    )
    out_specs = (P(None, "col"), P(None, "col"))
    return jax.shard_map(
        per_device, mesh=mesh, in_specs=in_specs, out_specs=out_specs, check_vma=False
    )
```

```python
import functools

import jax
import jax.numpy as jnp
from jax import lax
from jax.experimental import pallas as pl
from jax.experimental.pallas import tpu as pltpu
from jax.sharding import PartitionSpec as P

TILE = 64
CHUNK = 1024
LAYER = 8
F32 = jnp.float32
BF16 = jnp.bfloat16
MESH = pl.DeviceIdType.MESH


def iota(shape, dim):
    return lax.broadcasted_iota(jnp.int32, shape, dim)


def dot(a, b):
    return jnp.dot(a, b, preferred_element_type=F32)


def dot_tn(a, b):
    return lax.dot_general(a, b, (((0,), (0,)), ((), ())), preferred_element_type=F32)


def dot_nt(a, b):
    return lax.dot_general(a, b, (((1,), (1,)), ((), ())), preferred_element_type=F32)


def ones_where(mask):
    return jnp.where(mask, 1.0, 0.0).astype(BF16)


def kernel(
    cfg,
    neigh_ref,
    inc_hbm,
    ens_hbm,
    clim_hbm,
    rd_hbm,
    rl_hbm,
    rw_hbm,
    conv_hbm,
    id_hbm,
    il_hbm,
    iw_hbm,
    once_hbm,
    twice_hbm,
    inc_ref,
    ens_ref,
    clim_ref,
    rd_ref,
    rl_ref,
    rw_ref,
    conv_ref,
    id_ref,
    il_ref,
    iw_ref,
    once_ref,
    twice_ref,
    sum_ref,
    spread_ref,
    pack_ref,
    unpack_ref,
    gather_ref,
    choose_ref,
    partial_ref,
    value_ref,
    a1_send,
    a1_recv,
    ext_first,
    ext_second,
    a2_send,
    a2_recv,
    rs_send,
    rs_recv,
    own_ref,
    ag_send,
    ag_recv,
    ens_sem,
    in_sem,
    out_sem,
    a1_ssem,
    a1_rsem,
    halo_ssem,
    halo_rsem,
    a2_ssem,
    a2_rsem,
    rs_ssem,
    rs_rsem,
    ag_ssem,
    ag_rsem,
):
    n_col, n_mem, members, levels, fine, cap, scale = cfg
    tiles = fine // TILE
    feature = members * levels
    part = fine // n_mem
    part_tiles = part // TILE
    cap2 = 2 * cap
    slots1 = n_col * cap
    slots2 = n_col * cap2
    me = lax.axis_index("col")
    my_mem = lax.axis_index("mem")
    right = lax.rem(me + 1, n_col)
    left = lax.rem(me + n_col - 1, n_col)

    layers = n_col // LAYER
    my_layer = me // LAYER
    my_place = lax.rem(me, LAYER)
    far_first = sorted(range(layers), key=lambda dz: -min(dz, layers - dz))

    def ens_load(q):
        cols = pl.ds(q * part, part)
        return pltpu.make_async_copy(
            ens_hbm.at[:, :, cols], ens_ref.at[:, :, cols], ens_sem.at[q]
        )

    loads = [
        pltpu.make_async_copy(src, dst, in_sem.at[i])
        for i, (src, dst) in enumerate(
            (
                (rd_hbm, rd_ref),
                (rw_hbm, rw_ref),
                (inc_hbm, inc_ref),
                (rl_hbm, rl_ref),
                (id_hbm, id_ref),
                (il_hbm, il_ref),
                (conv_hbm, conv_ref),
                (iw_hbm, iw_ref),
                (clim_hbm, clim_ref),
            )
        )
    ]
    for load in loads[:3]:
        load.start()
    for q in range(n_mem):
        ens_load(q).start()
    barrier = pltpu.get_barrier_semaphore()
    for dz in far_first:

        @pl.loop(0 if dz else 1, LAYER)
        def _(i, dz=dz):
            peer = lax.rem(my_layer + dz, layers) * LAYER + lax.rem(my_place + i, LAYER)
            pl.semaphore_signal(
                barrier, inc=1, device_id=(my_mem, peer), device_id_type=MESH
            )

    for i in range(1, n_mem):
        pl.semaphore_signal(
            barrier, inc=1, device_id=(lax.rem(my_mem + i, n_mem), me), device_id_type=MESH
        )

    for load in loads[3:]:
        load.start()

    chunk_tiles = CHUNK // TILE
    per = part // CHUNK
    sum_ref[...] = ones_where(
        (iota((chunk_tiles, CHUNK), 1) >> 6) == iota((chunk_tiles, CHUNK), 0)
    )

    half = tiles // 2
    loads[0].wait()
    owner = jnp.concatenate(
        [rd_ref[pl.ds(2 * me, 1), :], rd_ref[pl.ds(2 * me + 1, 1), :]], axis=1
    )
    slot_row = iota((slots1, tiles), 0)
    named = slot_row // cap == owner
    before = dot(
        ones_where(named), ones_where(iota((tiles, tiles), 0) < iota((tiles, tiles), 1))
    )
    pack_ref[...] = ones_where(named & (before == (slot_row % cap).astype(F32)))

    def columns(chunk):
        return pl.ds(pl.multiple_of(chunk * CHUNK, CHUNK), CHUNK)

    def restrict(state, chunk):
        cols = columns(chunk)
        w = state * rw_ref[:, cols]
        prod = jnp.concatenate(
            [ens_ref[m, :, cols].astype(F32) * w for m in range(members)], axis=0
        ).astype(BF16)
        partial_ref[chunk] = dot_nt(sum_ref[...], prod).astype(BF16)

    def all_to_all(block, src, dst, ssem, rsem):
        for dz in far_first:
            layer = lax.rem(my_layer + dz, layers)
            if block is not None:
                src[pl.ds(layer * LAYER, LAYER)] = block(layer)

            def send(i, carry, dz=dz, layer=layer):
                peer = layer * LAYER + lax.rem(my_place + 4 + i, LAYER)
                pltpu.make_async_remote_copy(
                    src_ref=src.at[peer],
                    dst_ref=dst.at[me],
                    send_sem=ssem,
                    recv_sem=rsem,
                    device_id=(my_mem, peer),
                    device_id_type=MESH,
                ).start()
                return carry

            if dz:
                lax.fori_loop(0, LAYER, send, 0, unroll=True)
            else:
                lax.fori_loop(0, 4, send, 0, unroll=True)
                lax.fori_loop(5, LAYER, send, 0, unroll=True)
        dst[me] = src[me]

    def wait_blocks(ref, sem):
        some = ref.at[pl.ds(0, n_col - 1)]
        pltpu.make_async_copy(some, some, sem).wait()

    def nodes_of(mask, local, group, groups, width, start, size, many):
        def halves(values):
            found = []
            for g in group:
                column = iota((values.shape[0], width), 1) + start
                spread = ones_where(
                    iota((values.shape[0], width), 0) == column // size * groups + g
                )
                found.append(dot_tn(values, spread))
            return jnp.concatenate(found, axis=0)

        mine = halves(mask)
        names = halves(local)
        lower = ones_where(iota((many, many), 1) < iota((many, many), 0))
        before = dot(lower, mine.astype(BF16))
        slot = ((iota((many, width), 1) + start) % size).astype(F32)
        hit = jnp.where(before == slot, mine, 0.0)
        node = jnp.sum(hit * names, axis=0, keepdims=True)
        filled = jnp.sum(hit, axis=0, keepdims=True)
        node = jnp.where(filled > 0.5, node, -1.0)
        return jnp.where(iota((tiles, width), 0).astype(F32) == node, 1.0, 0.0)

    def build_unpack():
        loads[3].wait()
        unpack_ref[...] = nodes_of(
            ones_where(rd_ref[...] == me),
            rl_ref[...].astype(F32).astype(BF16),
            (0, 1),
            2,
            slots1,
            0,
            cap,
            tiles,
        ).astype(BF16)

    def build_gather():
        width = 256
        loads[4].wait()
        loads[5].wait()
        mask = ones_where(id_ref[...] == me)
        local = il_ref[...].astype(F32).astype(BF16)
        for b in range(slots2 // width):
            block = nodes_of(
                mask, local, (0, 2, 1, 3), 4, width, b * width, cap2, 2 * tiles
            )
            gather_ref[pl.ds(b * width, width), :] = block.T.astype(BF16)

    def build_choose():
        width = 256
        pairs = 2 * tiles
        target = jnp.concatenate(
            [id_ref[pl.ds(4 * me + g, 1), :] for g in (0, 2, 1, 3)], axis=1
        )
        upper = ones_where(iota((pairs, pairs), 0) < iota((pairs, pairs), 1))
        for b in range(slots2 // width):
            slot_row = iota((width, pairs), 0) + b * width
            named = slot_row // cap2 == target
            before = dot(ones_where(named), upper)
            block = jnp.where(
                named & (before == (slot_row % cap2).astype(F32)), 1.0, 0.0
            )
            block = block.T.astype(BF16)
            for q in range(n_mem):
                for k in range(2):
                    at = k * tiles + q * part_tiles
                    choose_ref[q, pl.ds(k * part_tiles, part_tiles), pl.ds(b * width, width)] = (
                        block[at : at + part_tiles]
                    )

    def build_spread():
        @pl.loop(0, n_mem * per)
        def _(i):
            q = i // per
            c = lax.rem(i, per)
            shape = (part_tiles, CHUNK)
            mask = ((iota(shape, 1) + c * CHUNK) >> 6) == iota(shape, 0)
            for k in range(2):
                spread_ref[q, pl.ds(k * part_tiles, part_tiles), columns(c)] = jnp.where(
                    mask, iw_ref[pl.ds(k, 1), columns(i)], 0.0
                ).astype(BF16)

    def member_sum(q, c):
        interp = dot(value_ref[q], spread_ref[q, :, columns(c)])
        cols = columns(q * per + c)
        total = ens_ref[0, :, cols].astype(F32) * interp[0:levels]
        for m in range(1, members):
            total += ens_ref[m, :, cols].astype(F32) * interp[m * levels : (m + 1) * levels]
        return total

    def wait_all(ref, sem):
        pltpu.make_async_copy(ref, ref, sem).wait()

    for app in range(2):
        old_ref, new_ref, new_hbm = (
            (inc_ref, once_ref, once_hbm) if app == 0 else (once_ref, twice_ref, twice_hbm)
        )
        if app == 0:
            loads[1].wait()
            loads[2].wait()
            for q in range(n_mem):
                ens_load(q).wait()

                def first(c, carry, q=q):
                    chunk = q * per + c
                    restrict(inc_ref[:, columns(chunk)], chunk)
                    return carry

                lax.fori_loop(0, per, first, 0, unroll=2)
        partial = partial_ref[...].reshape(tiles, feature)

        outgoing = dot(pack_ref[...], partial)
        a1_send[app] = outgoing.reshape(n_col, cap, feature).astype(BF16)

        if app == 0:
            pl.semaphore_wait(barrier, n_col - 1 + n_mem - 1)
        all_to_all(None, a1_send.at[app], a1_recv.at[app], a1_ssem.at[app], a1_rsem.at[app])
        if app == 0:
            build_unpack()
        wait_blocks(a1_recv.at[app], a1_rsem.at[app])
        ext_ref = ext_first if app == 0 else ext_second
        incoming = a1_recv[app].astype(F32).reshape(slots1, feature).astype(BF16)
        coarse = dot(unpack_ref[...], incoming).astype(BF16)
        ext_ref[2:4] = coarse.reshape(2, tiles // 2, feature)
        halos = []
        for side, peer, at in ((0, right, 0), (1, left, 4)):
            halo = pltpu.make_async_remote_copy(
                src_ref=ext_ref.at[pl.ds(2, 2)],
                dst_ref=ext_ref.at[pl.ds(at, 2)],
                send_sem=halo_ssem.at[app, side],
                recv_sem=halo_rsem.at[app, side],
                device_id=(my_mem, peer),
                device_id_type=MESH,
            )
            halo.start()
            halos.append(halo)
        if app == 0:
            build_gather()
            loads[6].wait()
        for halo in halos:
            halo.wait_recv()
        nodes = []
        for b in range(2):
            total = None
            for k in range(4):
                block = lax.rem(
                    neigh_ref[b, k] - (me - 1) * 2 + 4 * n_col, 2 * n_col
                )
                term = dot(conv_ref[b, k], ext_ref[jnp.minimum(block, 5)])
                total = term if total is None else total + term
            nodes.append(total.astype(BF16))
        nodes = jnp.concatenate(nodes, axis=0)

        def replies(layer):
            rows = LAYER * cap2
            at = pl.ds(pl.multiple_of(layer * rows, rows), rows)
            return dot(gather_ref[at, :], nodes).astype(BF16).reshape(LAYER, cap2, feature)

        all_to_all(replies, a2_send.at[app], a2_recv.at[app], a2_ssem.at[app], a2_rsem.at[app])
        if app == 0:
            build_choose()
            loads[7].wait()
            build_spread()
            loads[8].wait()
        wait_blocks(a2_recv.at[app], a2_rsem.at[app])
        answers = a2_recv[app].reshape(slots2, feature)

        def fetch(q):
            value_ref[q] = dot(choose_ref[q], answers).T.astype(BF16)

        for i in (2, 1, 3):
            fetch(lax.rem(my_mem + i, n_mem))

        @pl.loop(0, per)
        def _(c):
            pieces = []
            for i in (2, 1, 3):
                pieces.append((i, member_sum(lax.rem(my_mem + i, n_mem), c)))
            for i, piece in pieces:
                rs_send[app, c, i - 1] = piece.astype(BF16)
                pltpu.make_async_remote_copy(
                    src_ref=rs_send.at[app, c, i - 1],
                    dst_ref=rs_recv.at[app, c, i - 1],
                    send_sem=rs_ssem.at[app],
                    recv_sem=rs_rsem.at[app, c],
                    device_id=(lax.rem(my_mem + i, n_mem), me),
                    device_id_type=MESH,
                ).start()

        fetch(my_mem)

        @pl.loop(0, per)
        def _(c):
            own_ref[c] = member_sum(my_mem, c)

        @pl.loop(0, per)
        def _(c):
            wait_all(rs_recv.at[app, c], rs_rsem.at[app, c])
            total = own_ref[c]
            for i in range(n_mem - 1):
                total += rs_recv[app, c, i].astype(F32)
            ag_send[app, c] = total.astype(BF16)
            for i in (2, 1, 3):
                pltpu.make_async_remote_copy(
                    src_ref=ag_send.at[app, c],
                    dst_ref=ag_recv.at[app, c, i - 1],
                    send_sem=ag_ssem.at[app],
                    recv_sem=ag_rsem.at[app, c],
                    device_id=(lax.rem(my_mem + i, n_mem), me),
                    device_id_type=MESH,
                ).start()

        def finish(q, c, summed):
            chunk = q * per + c
            cols = columns(chunk)
            state = clim_ref[:, cols] * old_ref[:, cols] + summed.astype(F32) * scale
            new_ref[:, cols] = state
            pltpu.make_async_copy(
                new_ref.at[:, cols], new_hbm.at[:, cols], out_sem.at[app]
            ).start()
            if app == 0:
                restrict(state, chunk)

        def finish_own(c, carry):
            finish(my_mem, c, ag_send[app, c])
            return carry

        lax.fori_loop(0, per, finish_own, 0, unroll=2)

        @pl.loop(0, per)
        def _(c):
            wait_all(ag_recv.at[app, c], ag_rsem.at[app, c])
            for i in (1, 3, 2):
                finish(lax.rem(my_mem + n_mem - i, n_mem), c, ag_recv[app, c, i - 1])

        wait_all(rs_send.at[app], rs_ssem.at[app])
        wait_all(ag_recv.at[app], ag_ssem.at[app])
        for halo in halos:
            halo.wait_send()

    for app in range(2):
        wait_blocks(a1_send.at[app], a1_ssem.at[app])
        wait_blocks(a2_send.at[app], a2_ssem.at[app])
        wait_all((once_ref, twice_ref)[app], out_sem.at[app])


def result_kernel(once_in, twice_in, once_out, twice_out, once_ref, twice_ref, sem):
    pieces = 4
    width = once_ref.shape[1] // pieces
    pairs = []
    for k, (src, ref, dst) in enumerate(
        ((once_in, once_ref, once_out), (twice_in, twice_ref, twice_out))
    ):
        for p in range(pieces):
            cols = pl.ds(p * width, width)
            pairs.append(
                (
                    pltpu.make_async_copy(src.at[:, cols], ref.at[:, cols], sem.at[0, k, p]),
                    pltpu.make_async_copy(ref.at[:, cols], dst.at[:, cols], sem.at[1, k, p]),
                )
            )
    for load, _ in pairs:
        load.start()
    for load, store in pairs:
        load.wait()
        store.start()
    for _, store in pairs:
        store.wait()


def per_device(
    increment,
    ensemble,
    climate,
    restrict_dest,
    restrict_local,
    restrict_weight,
    conv_blocks,
    neighbours,
    interp_dest,
    interp_local,
    interp_weight,
):
    n_col = lax.axis_size("col")
    n_mem = lax.axis_size("mem")
    members, levels, fine = ensemble.shape
    tiles = fine // TILE
    part = fine // n_mem
    part_tiles = part // TILE
    per = part // CHUNK
    feature = members * levels
    cap = max(2, 2 * tiles // n_col)
    scale = 1.0 / (members * n_mem - 1)
    cfg = (n_col, n_mem, members, levels, fine, cap, scale)

    blocks = n_col * tiles // 128

    def pairs(a):
        return a.T.reshape(2, blocks, 128).transpose(1, 0, 2).reshape(2 * blocks, 128)

    smem = pl.BlockSpec(memory_space=pltpu.SMEM)
    hbm = pl.BlockSpec(memory_space=pl.ANY)
    dma = pltpu.SemaphoreType.DMA
    result = jax.ShapeDtypeStruct((levels, fine), F32)
    once, twice = pl.pallas_call(
        functools.partial(kernel, cfg),
        out_shape=(result, result),
        in_specs=[smem] + [hbm] * 10,
        out_specs=(hbm, hbm),
        scratch_shapes=[
            pltpu.VMEM((levels, fine), F32),
            pltpu.VMEM((members, levels, fine), BF16),
            pltpu.VMEM((levels, fine), F32),
            pltpu.VMEM((blocks, 128), jnp.int32),
            pltpu.VMEM((blocks, 128), jnp.int32),
            pltpu.VMEM((1, fine), F32),
            pltpu.VMEM(conv_blocks.shape, BF16),
            pltpu.VMEM((2 * blocks, 128), jnp.int32),
            pltpu.VMEM((2 * blocks, 128), jnp.int32),
            pltpu.VMEM((2, fine), F32),
            pltpu.VMEM((levels, fine), F32),
            pltpu.VMEM((levels, fine), F32),
            pltpu.VMEM((CHUNK // TILE, CHUNK), BF16),
            pltpu.VMEM((n_mem, 2 * part_tiles, part), BF16),
            pltpu.VMEM((n_col * cap, tiles), BF16),
            pltpu.VMEM((tiles, n_col * cap), BF16),
            pltpu.VMEM((n_col * 2 * cap, tiles), BF16),
            pltpu.VMEM((n_mem, 2 * part_tiles, n_col * 2 * cap), BF16),
            pltpu.VMEM((fine // CHUNK, CHUNK // TILE, feature), BF16),
            pltpu.VMEM((n_mem, feature, 2 * part_tiles), BF16),
            pltpu.VMEM((2, n_col, cap, feature), BF16),
            pltpu.VMEM((2, n_col, cap, feature), BF16),
            pltpu.VMEM((6, tiles // 2, feature), BF16),
            pltpu.VMEM((6, tiles // 2, feature), BF16),
            pltpu.VMEM((2, n_col, 2 * cap, feature), BF16),
            pltpu.VMEM((2, n_col, 2 * cap, feature), BF16),
            pltpu.VMEM((2, per, n_mem - 1, levels, CHUNK), BF16),
            pltpu.VMEM((2, per, n_mem - 1, levels, CHUNK), BF16),
            pltpu.VMEM((per, levels, CHUNK), F32),
            pltpu.VMEM((2, per, levels, CHUNK), BF16),
            pltpu.VMEM((2, per, n_mem - 1, levels, CHUNK), BF16),
            dma((n_mem,)),
            dma((9,)),
            dma((2,)),
            dma((2,)),
            dma((2,)),
            dma((2, 2)),
            dma((2, 2)),
            dma((2,)),
            dma((2,)),
            dma((2,)),
            dma((2, per)),
            dma((2,)),
            dma((2, per)),
        ],
        compiler_params=pltpu.CompilerParams(
            collective_id=0, has_side_effects=True, vmem_limit_bytes=60 * 1024 * 1024
        ),
        name="covariance_twice",
    )(
        neighbours,
        increment,
        ensemble,
        climate,
        restrict_dest.reshape(blocks, 128),
        restrict_local.reshape(blocks, 128),
        restrict_weight.reshape(1, fine),
        conv_blocks,
        pairs(interp_dest),
        pairs(interp_local),
        interp_weight,
    )
    return pl.pallas_call(
        result_kernel,
        out_shape=(result, result),
        in_specs=[hbm, hbm],
        out_specs=(hbm, hbm),
        scratch_shapes=[
            pltpu.VMEM((levels, fine), F32),
            pltpu.VMEM((levels, fine), F32),
            dma((2, 2, 4)),
        ],
        compiler_params=pltpu.CompilerParams(vmem_limit_bytes=60 * 1024 * 1024),
        name="results",
    )(once, twice)


def solution(mesh):
    in_specs = (
        P(None, "col"),
        P("mem", None, "col"),
        P(None, "col"),
        P(),
        P(),
        P("col"),
        P("col", None, None, None),
        P("col", None),
        P(),
        P(),
        P(None, "col"),
    )
    out_specs = (P(None, "col"), P(None, "col"))
    return jax.shard_map(
        per_device, mesh=mesh, in_specs=in_specs, out_specs=out_specs, check_vma=False
    )
```
